32 devices in a mesh: slab: 4 (over x, core), space: 8 (over z, y).
Axes of the slice: x: 2, y: 2, z: 4, core: 2. Of those that a mesh axis runs over, the one named last changes fastest.
Arguments:
- forcing: float32 [8, 3, 4, 4, 4, 8192], P('slab', None, None, None, None, 'space'), may hold values from -6 to 6
- coefficient: float32 [8192], P('space'), may hold values from 1.5 to 4
- neighbours: int32 [6, 8192], P(None, 'space'), may hold values from 0 to 2048, as said below
- halo_faces: int32 [2, 4096], P(None, 'space'), may hold values from 0 to 1023, as said below
- time_block: float32 [3, 3], replicated, may hold values from -0.6 to 1.6
- space_block: float32 [4, 4], replicated, may hold values from -0.6 to 1.6
- stiffness: float32 [4, 4], replicated, may hold values from -0.6 to 0.6
- time_restrict: float32 [1, 3], replicated, may hold values from 0.5 to 1.5
- space_restrict: float32 [2, 4], replicated, may hold values from 0.5 to 1.5
- coarse_smoother: float32 [2, 2], replicated, may hold values from -0.8 to 1.8
Outputs:
- correction: float32 [8, 3, 4, 4, 4, 8192], P('slab', None, None, None, None, 'space')
The draws below stay inside these ranges and needn't reach their ends.
Inputs may be any that keep to these rules, and one draw needn't show every extreme that they name: `neighbours`: for element e of partition p (local numbers below 1024) and face f = -x, +x, -y, +y, -z, +z in that order: a local element of p whose opposite face is the same face with the same node order, or 1024 + m for the m-th element of the left partition's rightward list (row 1 of halo_faces), or 1536 + m for the m-th element of the right partition's leftward list (row 0), or 2048 where the face lies on the domain boundary. Ghost slots appear only for the -x face (left) and the +x face (right). `halo_faces`: row 0 lists, in local numbers, the 512 elements of a partition whose -x face touches the left partition, row 1 those whose +x face touches the right partition, each once.
All inputs are finite; a program needn't handle non-finite values.
Results may differ from the reference program's by a relative error of at most 0.00027.
Values sent between devices are 32-bit elements; how exact they have to be, the bound alone decides.
No kernel may reach another device: no remote copies, remote signals or barrier semaphores. Data moves between devices by JAX's collectives and lax.ppermute only.
A program may use at most 128 MiB of HBM per device.

```python
import math
import jax
import jax.numpy as jnp
from jax import lax

Q = 3
P_SIZE = 4
PC = 2
SWEEPS = 3
EX = 2
EY = 8
EZ = 64
E_DEV = 1024
GHOST = 512
SLABS = 8
ELEMS = 8192
N_SPACE = 8


def mesh_tables(key):
    key_mesh = jax.random.fold_in(key, 4242)
    parts = jnp.arange(N_SPACE, dtype=jnp.int32)

    def orders(part_index):
        part_key = jax.random.fold_in(key_mesh, part_index)
        sub_keys = jax.random.split(part_key, 3)
        numbering = jax.random.permutation(sub_keys[0], E_DEV).astype(jnp.int32)
        left_order = jax.random.permutation(sub_keys[1], GHOST).astype(jnp.int32)
        right_order = jax.random.permutation(sub_keys[2], GHOST).astype(jnp.int32)
        return (numbering, left_order, right_order)
    numbering, left_order, right_order = jax.vmap(orders)(parts)
    slots = jnp.arange(GHOST, dtype=jnp.int32)

    def invert(order_row):
        return jnp.zeros((GHOST,), jnp.int32).at[order_row].set(slots)
    left_slot = jax.vmap(invert)(left_order)
    right_slot = jax.vmap(invert)(right_order)
    cells = jnp.arange(E_DEV, dtype=jnp.int32)
    layer = cells // GHOST
    within = cells % GHOST
    row_index = within // EZ
    col_index = within % EZ
    boundary = E_DEV + 2 * GHOST

    def table(part_index):
        own = numbering[part_index]

        def neighbour_of(offset):
            return own[jnp.clip(cells + offset, 0, E_DEV - 1)]
        left_part = jnp.clip(part_index - 1, 0, N_SPACE - 1)
        right_part = jnp.clip(part_index + 1, 0, N_SPACE - 1)
        minus_x = jnp.where(layer > 0, neighbour_of(-GHOST), jnp.where(part_index > 0, E_DEV + right_slot[left_part][within], boundary))
        plus_x = jnp.where(layer < EX - 1, neighbour_of(GHOST), jnp.where(part_index < N_SPACE - 1, E_DEV + GHOST + left_slot[right_part][within], boundary))
        minus_y = jnp.where(row_index > 0, neighbour_of(-EZ), boundary)
        plus_y = jnp.where(row_index < EY - 1, neighbour_of(EZ), boundary)
        minus_z = jnp.where(col_index > 0, neighbour_of(-1), boundary)
        plus_z = jnp.where(col_index < EZ - 1, neighbour_of(1), boundary)
        by_cell = jnp.stack([minus_x, plus_x, minus_y, plus_y, minus_z, plus_z]).astype(jnp.int32)
        by_local = jnp.zeros((6, E_DEV), jnp.int32).at[:, own].set(by_cell)
        sends = jnp.stack([own[left_order[part_index]], own[(EX - 1) * GHOST + right_order[part_index]]])
        return (by_local, sends.astype(jnp.int32))
    tables, send_lists = jax.vmap(table)(parts)
    neighbour_table = jnp.transpose(tables, (1, 0, 2)).reshape(6, N_SPACE * E_DEV)
    face_lists = jnp.transpose(send_lists, (1, 0, 2)).reshape(2, N_SPACE * GHOST)
    return (neighbour_table.astype(jnp.int32), face_lists.astype(jnp.int32))


def draw_neighbours(key, part):
    return mesh_tables(key)[0]


def draw_halo_faces(key, part):
    return mesh_tables(key)[1]


def near_identity(key, order, spread):
    perturbation = spread * jnp.clip(jax.random.normal(key, (order, order), jnp.float32), -4.0, 4.0)
    return jnp.eye(order, dtype=jnp.float32) + perturbation


def draw_time_block(key, part):
    return near_identity(jax.random.fold_in(key, 11), Q, 0.15)


def draw_space_block(key, part):
    return near_identity(jax.random.fold_in(key, 12), P_SIZE, 0.15)


def draw_coarse_smoother(key, part):
    return near_identity(jax.random.fold_in(key, 13), PC, 0.2)


def levels(own_key, shape, shards, least, top_value):
    def one(dim, blocks):
        steps = jax.random.uniform(jax.random.fold_in(jax.random.fold_in(own_key, 6), dim), (blocks,), jnp.float32, least / len(shards), top_value / len(shards))
        return jnp.repeat(jnp.exp(steps), shape[dim] // blocks).reshape((-1,) + (1,) * (len(shape) - dim - 1))

    gain = one(*shards[0])
    for cut in shards[1:]:
        gain = gain * one(*cut)
    return gain


def noise(stream_key, dims, scale, reach, cuts=(), kind=jnp.bfloat16):
    factor_of = levels(stream_key, dims, cuts, -0.22, 0.18) if cuts else 1.0
    values = jax.random.normal(stream_key, dims, jnp.float32) * scale * factor_of
    return jnp.minimum(jnp.maximum(values, -reach), reach).astype(kind)


def setup_inputs(seed: int = 0) -> dict:
    keys = jax.random.split(jax.random.key(seed), 11)
    forcing = noise(keys[0], (SLABS, Q, P_SIZE, P_SIZE, P_SIZE, ELEMS), 1.0, 6.0, ((0, 4), (5, 8)), jnp.float32)
    coefficient = jnp.clip(jnp.exp(math.log(4.0) - 0.98082925 * jax.random.uniform(keys[1], (ELEMS,), jnp.float32) ** levels(keys[1], (ELEMS,), ((0, 8),), -0.2, 0.2)), 1.5, 4.0)
    neighbours = draw_neighbours(jax.random.fold_in(keys[10], 71), 0)
    halo_faces = draw_halo_faces(jax.random.fold_in(keys[10], 71), 0)
    time_block = draw_time_block(jax.random.fold_in(keys[10], 71), 0)
    space_block = draw_space_block(jax.random.fold_in(keys[10], 71), 0)
    stiffness = noise(keys[6], (P_SIZE, P_SIZE), 0.1, 0.6, (), jnp.float32)
    time_restrict = jnp.clip(jax.random.uniform(keys[7], (1, Q), jnp.float32, 0.5, 1.5), 0.5, 1.5)
    space_restrict = jnp.clip(jax.random.uniform(keys[8], (PC, P_SIZE), jnp.float32, 0.5, 1.5), 0.5, 1.5)
    coarse_smoother = draw_coarse_smoother(jax.random.fold_in(keys[10], 71), 0)
    return {"forcing": forcing, "coefficient": coefficient, "neighbours": neighbours, "halo_faces": halo_faces, "time_block": time_block, "space_block": space_block, "stiffness": stiffness, "time_restrict": time_restrict, "space_restrict": space_restrict, "coarse_smoother": coarse_smoother}


HIGHEST_PRECISION = lax.Precision.HIGHEST
PENALTY = 0.3
UPWIND = 0.5
COARSE_UPWIND = 0.6


def apply_along(matrix, field_in, dim_index):
    letters = "abcdefgh"[:field_in.ndim]
    source = letters[:dim_index] + "q" + letters[dim_index + 1:]
    target = letters[:dim_index] + "p" + letters[dim_index + 1:]
    return jnp.einsum("pq," + source + "->" + target, matrix, field_in, precision=HIGHEST_PRECISION)


def space_apply(space_matrix, field_in, first_dim):
    result = field_in
    for dim_index in (first_dim, first_dim + 1, first_dim + 2):
        result = apply_along(space_matrix, result, dim_index)
    return result


def kron_apply(time_matrix, space_matrix, field_in):
    return space_apply(space_matrix, apply_along(time_matrix, field_in, 1), 2)


def stiffness_apply(stiffness, field_in):
    summed = apply_along(stiffness, field_in, 2) + apply_along(stiffness, field_in, 3)
    return summed + apply_along(stiffness, field_in, 4)


def face_trace(field_in, face_index):
    dim_index = 2 + face_index // 2
    node_index = (face_index % 2) * (field_in.shape[dim_index] - 1)
    return lax.index_in_dim(field_in, node_index, dim_index, keepdims=False)


def add_layer(field_in, values, face_index):
    dim_index = 2 + face_index // 2
    node_index = (face_index % 2) * (field_in.shape[dim_index] - 1)
    position = (slice(None),) * dim_index + (node_index,)
    return field_in.at[position].add(values)


def jacobi(values, coefficient, time_block, space_block):
    time_inverse = 2.0 * jnp.eye(time_block.shape[0], dtype=jnp.float32) - time_block
    space_inverse = 2.0 * jnp.eye(space_block.shape[0], dtype=jnp.float32) - space_block
    return kron_apply(time_inverse, space_inverse, values) / coefficient


def source_table(neighbours, halo_faces):
    elements = jnp.arange(ELEMS, dtype=jnp.int32)
    partition = elements // E_DEV
    left_part = jnp.clip(partition - 1, 0, N_SPACE - 1)
    right_part = jnp.clip(partition + 1, 0, N_SPACE - 1)
    left_slot = jnp.clip(neighbours - E_DEV, 0, GHOST - 1)
    right_slot = jnp.clip(neighbours - E_DEV - GHOST, 0, GHOST - 1)
    from_left = left_part * E_DEV + halo_faces[1][left_part * GHOST + left_slot]
    from_right = right_part * E_DEV + halo_faces[0][right_part * GHOST + right_slot]
    local_source = partition * E_DEV + jnp.clip(neighbours, 0, E_DEV - 1)
    outside = jnp.full(neighbours.shape, ELEMS, jnp.int32)
    sources = jnp.where(neighbours < E_DEV + 2 * GHOST, from_right, outside)
    sources = jnp.where(neighbours < E_DEV + GHOST, from_left, sources)
    sources = jnp.where(neighbours < E_DEV, local_source, sources)
    return sources.astype(jnp.int32)


def operate(field_in, coefficient, sources, time_block, space_block, stiffness):
    result = coefficient * kron_apply(time_block, space_block, field_in) + stiffness_apply(stiffness, field_in)
    for face_index in range(6):
        face_values = face_trace(field_in, face_index ^ 1)
        padded = jnp.concatenate([face_values, jnp.zeros(face_values.shape[:-1] + (1,), jnp.float32)], axis=-1)
        coupled = jnp.take(padded, sources[face_index], axis=-1)
        result = add_layer(result, -PENALTY * coupled, face_index)
    previous = jnp.concatenate([jnp.zeros((1,) + field_in.shape[2:], jnp.float32), field_in[:-1, -1]], axis=0)
    return result.at[:, 0].add(-UPWIND * coefficient * previous)


def reference(forcing, coefficient, neighbours, halo_faces, time_block, space_block, stiffness, time_restrict, space_restrict, coarse_smoother):
    sources = source_table(neighbours, halo_faces)
    iterate = jacobi(forcing, coefficient, time_block, space_block)
    for sweep_index in range(SWEEPS - 1):
        applied = operate(iterate, coefficient, sources, time_block, space_block, stiffness)
        iterate = iterate + jacobi(forcing - applied, coefficient, time_block, space_block)
    residual = forcing - operate(iterate, coefficient, sources, time_block, space_block, stiffness)
    coarse = kron_apply(time_restrict, space_restrict, residual)
    grouped = coarse[0::2] + coarse[1::2]

    def advance(carry_state, group_values):
        new_state = space_apply(coarse_smoother, COARSE_UPWIND * carry_state + group_values / coefficient, 1)
        return new_state, new_state

    initial = jnp.zeros(grouped.shape[1:], jnp.float32)
    final_state, states = lax.scan(advance, initial, grouped)
    spread = jnp.repeat(states, 2, axis=0)
    return iterate + kron_apply(time_restrict.T, space_restrict.T, spread)
```

```python
import functools

import jax
import jax.numpy as jnp
from jax import lax
from jax.experimental import pallas as pl
from jax.experimental.pallas import tpu as pltpu
from jax.sharding import PartitionSpec as P

SWEEPS = 3
PENALTY = 0.3
UPWIND = 0.5
COARSE_UPWIND = 0.6
F32 = jnp.float32
BF16 = jnp.bfloat16
VMEM_BYTES = 56 * 1024 * 1024


def exact(a, b):
    return jnp.dot(a, b, precision=lax.Precision.HIGHEST, preferred_element_type=F32)


def iota(shape, dim):
    return lax.broadcasted_iota(jnp.int32, shape, dim)


def expand(small, rows, row_digit, cols, col_digit):
    n, m = small.shape
    left = (row_digit(iota((rows, n), 0)) == iota((rows, n), 1)).astype(F32)
    right = (iota((m, cols), 0) == col_digit(iota((m, cols), 1))).astype(F32)
    return exact(exact(left, small), right)


class Nodes:
    def __init__(self, q, p, pc):
        self.q, self.p, self.pc = q, p, pc
        self.n = q * p**3
        self.nc = pc**3
        self.nf = 6 * pc**2

    def fine(self, d):
        p = self.p
        if d == 0:
            return lambda r: r // p**3
        return lambda r: (r // p ** (3 - d)) % p

    def coarse(self, d):
        pc = self.pc
        return lambda r: (r // pc ** (3 - d)) % pc

    def face(self, r):
        return r // self.pc**2

    def bit(self, d, r):
        pc = self.pc
        high, low = (r // pc) % pc, r % pc
        if d == 1:
            return high
        if d == 3:
            return low
        return jnp.where(self.face(r) // 2 == 0, high, low)

    def fine_fine(self, small, d):
        return expand(small, self.n, self.fine(d), self.n, self.fine(d))

    def kron(self, time, x, y, z):
        return self.fine_fine(time, 0) * self.fine_fine(x, 1) * self.fine_fine(y, 2) * self.fine_fine(z, 3)

    def restricted(self, time, x, y, z):
        total = expand(time, self.nc, lambda r: r * 0, self.n, self.fine(0))
        for d, small in ((1, x), (2, y), (3, z)):
            total = total * expand(small, self.nc, self.coarse(d), self.n, self.fine(d))
        return total

    def prolonged(self, time_t, space_t):
        total = expand(time_t, self.n, self.fine(0), self.nc, lambda r: r * 0)
        for d in (1, 2, 3):
            total = total * expand(space_t, self.n, self.fine(d), self.nc, self.coarse(d))
        return total

    def coarse_coarse(self, small):
        total = 1.0
        for d in (1, 2, 3):
            total = total * expand(small, self.nc, self.coarse(d), self.nc, self.coarse(d))
        return total

    def face_traces(self, time, space):
        shape = (self.nf, self.n)
        row, col = iota(shape, 0), iota(shape, 1)
        face = self.face(row)
        opposite = jnp.where(face % 2 == 0, self.p - 1, 0)
        total = expand(time, self.nf, lambda r: r * 0, self.n, self.fine(0))
        for d in (1, 2, 3):
            tangential = expand(space, self.nf, functools.partial(self.bit, d), self.n, self.fine(d))
            normal = (self.fine(d)(col) == opposite).astype(F32)
            total = total * jnp.where(face // 2 == d - 1, normal, tangential)
        return total

    def face_spread(self, space):
        shape = (self.nc, self.nf)
        row, col = iota(shape, 0), iota(shape, 1)
        face = self.face(col)
        total = 1.0
        node = lambda r: jnp.where(self.face(r) % 2 == 0, 0, self.p - 1)
        for d in (1, 2, 3):
            normal = expand(space, self.nc, self.coarse(d), self.nf, node)
            tangential = (self.coarse(d)(row) == self.bit(d, col)).astype(F32)
            total = total * jnp.where(face // 2 == d - 1, normal, tangential)
        return total


def two_minus(small):
    n = small.shape[0]
    return 2.0 * (iota((n, n), 0) == iota((n, n), 1)).astype(F32) - small


def pieces(v):
    high = v.astype(BF16)
    return high, (v - high.astype(F32)).astype(BF16)


def bdot(a, b):
    return jnp.dot(a, b, preferred_element_type=F32)


def product(matrix, values):
    mh, ml = matrix
    vh, vl = values
    return bdot(mh, vh) + (bdot(mh, vl) + bdot(ml, vh))


def select_columns(values, indices, count):
    rows = values.shape[0]
    high, low = pieces(values)
    chosen = (iota((count, indices.shape[-1]), 0) == indices).astype(F32).astype(BF16)
    both = bdot(jnp.concatenate([high, low], axis=0), chosen)
    return both[:rows] + both[rows:]


def lower_half(shape):
    return iota(shape, 0) < 4


def trace_rows(ref, rows, face, p):
    d, node = face // 2, face % 2 * (p - 1)
    if d == 0:
        step = p * p
        return jnp.concatenate(
            [ref[r + node * step : r + (node + 1) * step, :] for r in range(0, rows, p * step)], axis=0
        )
    if d == 1:
        parts = []
        at = node * p // 8 * 8
        for r in range(0, rows, 2 * p * p):
            first = ref[r + at : r + at + 8, :]
            second = ref[r + p * p + at : r + p * p + at + 8, :]
            low = lower_half(first.shape)
            if node == 0:
                parts.append(jnp.where(low, first, pltpu.roll(second, 4, 0)))
            else:
                parts.append(jnp.where(low, pltpu.roll(first, 4, 0), second))
        return jnp.concatenate(parts, axis=0)
    raise ValueError(face)


def to_tiles(tiles_ref, ref):
    for k in range(tiles_ref.shape[0]):
        tiles_ref[k] = ref[:, 128 * k : 128 * k + 128]


def z_trace_rows(tiles_ref, rows, face, p):
    node = face % 2 * (p - 1)
    parts = [tiles_ref[k, pl.ds(node, rows // p, stride=p), :] for k in range(tiles_ref.shape[0])]
    return jnp.concatenate(parts, axis=1)


def z_put_rows(tiles_ref, values, rows, face, p):
    node = face % 2 * (p - 1)
    for k in range(tiles_ref.shape[0]):
        tiles_ref[k, pl.ds(node, rows // p, stride=p), :] = values[:, 128 * k : 128 * k + 128]


def add_rows(ref, values, rows, face, p):
    d, node = face // 2, face % 2 * (p - 1)
    if d == 0:
        step = p * p
        for i, r in enumerate(range(0, rows, p * step)):
            at = r + node * step
            ref[at : at + step, :] += values[i * step : (i + 1) * step]
    elif d == 1:
        at = node * p // 8 * 8
        for i, r in enumerate(range(0, rows, 2 * p * p)):
            eight = values[8 * i : 8 * i + 8]
            turned = pltpu.roll(eight, 4, 0)
            low = lower_half(eight.shape)
            if node == 0:
                first, second = jnp.where(low, eight, 0.0), jnp.where(low, turned, 0.0)
            else:
                first, second = jnp.where(low, 0.0, turned), jnp.where(low, 0.0, eight)
            ref[r + at : r + at + 8, :] += first
            ref[r + p * p + at : r + p * p + at + 8, :] += second


def last_time(nodes):
    return (nodes.q - 1) * nodes.p**3


def pack(x_ref, halo_ref, parity_ref, first_ref, second_ref, rows, p):
    elements = x_ref.shape[-1]
    to_left = select_columns(trace_rows(x_ref, rows, 0, p), halo_ref[0:1, :], elements)
    to_right = select_columns(trace_rows(x_ref, rows, 1, p), halo_ref[1:2, :], elements)
    even = parity_ref[0] == 0
    first_ref[...] = jnp.where(even, to_right, to_left)
    second_ref[...] = jnp.where(even, to_left, to_right)


def start_kernel(nodes, parity, f_ref, c_ref, halo_ref, tb, sb, tr, sr, x_ref, first_ref, second_ref, last_ref, rf_ref):
    n, p = nodes.n, nodes.p
    rows = f_ref.shape[0]
    ti, si = two_minus(tb[...]), two_minus(sb[...])
    inverse = pieces(nodes.kron(ti, si, si, si))
    scale = 1.0 / c_ref[...]
    total = 0.0
    for s in range(rows // n):
        f = f_ref[s * n : (s + 1) * n, :]
        total = total + f
        x_ref[s * n : (s + 1) * n, :] = product(inverse, pieces(f)) * scale
    pack(x_ref, halo_ref, parity, first_ref, second_ref, rows, p)
    at = rows - n + last_time(nodes)
    last_ref[...] = x_ref[at:rows, :]
    rf_ref[...] = product(pieces(nodes.restricted(tr[...], sr[...], sr[...], sr[...])), pieces(total))


def local_kernel(nodes, x_ref, x1_ref, c_ref, nb_ref, tb, sb, st, out_ref, g_ref, tiles_ref):
    n, p = nodes.n, nodes.p
    rows, elements = x_ref.shape
    plane = p**3
    ti, si = two_minus(tb[...]), two_minus(sb[...])
    tit, sis, sid = exact(ti, tb[...]), exact(si, sb[...]), exact(si, st[...])
    et = nodes.fine_fine(ti, 0)
    es = [nodes.fine_fine(si, d) for d in (1, 2, 3)]
    ed = [nodes.fine_fine(sid, d) for d in (1, 2, 3)]
    inverse = pieces(et * es[0] * es[1] * es[2])
    unit = (iota((n, n), 0) == iota((n, n), 1)).astype(F32)
    keep = pieces(unit - nodes.kron(tit, sis, sis, sis))
    drift = pieces(-et * (ed[0] * es[1] * es[2] + es[0] * ed[1] * es[2] + es[0] * es[1] * ed[2]))
    c = c_ref[...]
    scale = 1.0 / c
    g_ref[...] = jnp.zeros_like(g_ref)
    for s in range(1, rows // n):
        before = (s - 1) * n + last_time(nodes)
        g_ref[s * n : s * n + plane, :] = UPWIND * c * x_ref[before : before + plane, :]
    to_tiles(tiles_ref, x_ref)
    z_values = [z_trace_rows(tiles_ref, rows, face ^ 1, p) for face in (4, 5)]
    tiles_ref[...] = jnp.zeros_like(tiles_ref)
    for face in range(6):
        values = trace_rows(x_ref, rows, face ^ 1, p) if face < 4 else z_values[face - 4]
        coupled = PENALTY * select_columns(values, nb_ref[face : face + 1, :], elements)
        if face < 4:
            add_rows(g_ref, coupled, rows, face, p)
        else:
            z_put_rows(tiles_ref, coupled, rows, face, p)
    for k in range(tiles_ref.shape[0]):
        g_ref[:, 128 * k : 128 * k + 128] += tiles_ref[k]
    for s in range(rows // n):
        here = slice(s * n, (s + 1) * n)
        x = pieces(x_ref[here, :])
        turned = product(drift, x) + product(inverse, pieces(g_ref[here, :]))
        out_ref[here, :] = x1_ref[here, :] + product(keep, x) + scale * turned


def ghosts(parity_ref, got_first_ref, got_second_ref):
    even = parity_ref[0] == 0
    first, second = got_first_ref[...], got_second_ref[...]
    return jnp.where(even, second, first), jnp.where(even, first, second)


def finish(nodes, parity, base_ref, got_first, got_second, prev_a, prev_b, c_ref, nb_ref, tb, sb, x_ref, g_ref):
    n, p = nodes.n, nodes.p
    rows, elements = base_ref.shape
    ti, si = two_minus(tb[...]), two_minus(sb[...])
    inverse = pieces(nodes.kron(ti, si, si, si))
    c = c_ref[...]
    scale = 1.0 / c
    left, right = ghosts(parity, got_first, got_second)
    count = left.shape[-1]
    g_ref[...] = jnp.zeros_like(g_ref)
    g_ref[: p**3, :] = UPWIND * c * (prev_a[...] + prev_b[...])
    add_rows(g_ref, PENALTY * select_columns(left, nb_ref[0:1, :] - elements, count), rows, 0, p)
    add_rows(g_ref, PENALTY * select_columns(right, nb_ref[1:2, :] - (elements + count), count), rows, 1, p)
    for s in range(rows // n):
        here = slice(s * n, (s + 1) * n)
        x_ref[here, :] = base_ref[here, :] + scale * product(inverse, pieces(g_ref[here, :]))


def finish_kernel(
    nodes, parity, base_ref, got_first, got_second, prev_a, prev_b, c_ref, nb_ref, halo_ref, tb, sb,
    x_ref, first_ref, second_ref, last_ref, g_ref,
):
    finish(nodes, parity, base_ref, got_first, got_second, prev_a, prev_b, c_ref, nb_ref, tb, sb, x_ref, g_ref)
    rows = base_ref.shape[0]
    pack(x_ref, halo_ref, parity, first_ref, second_ref, rows, nodes.p)
    last_ref[...] = x_ref[rows - nodes.n + last_time(nodes) : rows, :]


def coarse_kernel(
    nodes, parity, base_ref, got_first, got_second, prev_a, prev_b, c_ref, nb_ref, halo_ref, rf_ref, tb, sb, st, tr, sr,
    x_ref, first_ref, second_ref, local_ref, g_ref,
):
    finish(nodes, parity, base_ref, got_first, got_second, prev_a, prev_b, c_ref, nb_ref, tb, sb, x_ref, g_ref)
    n, p, nc = nodes.n, nodes.p, nodes.nc
    rows, elements = x_ref.shape
    t, s = tr[...], sr[...]
    tk, sk, sd = exact(t, tb[...]), exact(s, sb[...]), exact(s, st[...])
    block = nodes.restricted(tk, sk, sk, sk)
    stiff = nodes.restricted(t, sd, s, s) + nodes.restricted(t, s, sd, s) + nodes.restricted(t, s, s, sd)
    faces = nodes.face_traces(t, s)
    stacked = pieces(jnp.concatenate([block, stiff, faces], axis=0))
    total = x_ref[:n, :]
    before = 0.0
    for k in range(1, rows // n):
        total = total + x_ref[k * n : (k + 1) * n, :]
        at = (k - 1) * n + last_time(nodes)
        before = before + x_ref[at : at + p**3, :]
    applied = product(stacked, pieces(total))
    first_node = pieces(nodes.restricted(t, s, s, s)[:, : p**3])
    c = c_ref[...]
    local = rf_ref[...] - c * applied[:nc] - applied[nc : 2 * nc]
    local = local + (UPWIND * c) * product(first_node, pieces(before))
    traces = applied[2 * nc :]
    high, low = pieces(traces)
    both = jnp.concatenate([high, low], axis=0)
    four = nodes.pc**2
    row = iota((nodes.nf, elements), 0) // four
    coupled = 0.0
    for face in range(6):
        chosen = (iota((elements, elements), 0) == nb_ref[face : face + 1, :]).astype(F32).astype(BF16)
        got = bdot(both, chosen)
        coupled = coupled + jnp.where(row == face, got[: nodes.nf] + got[nodes.nf :], 0.0)
    spread = nodes.face_spread(s)
    local_ref[:nc, :] = local + PENALTY * exact(spread, coupled)
    end = x_ref[rows - n + last_time(nodes) : rows, :]
    local_ref[nc:, :] = UPWIND * product(first_node, pieces(end))
    to_left = select_columns(traces[:8], halo_ref[0:1, :], elements)
    to_right = select_columns(traces[:8], halo_ref[1:2, :], elements)
    even = parity[0] == 0
    first_ref[...] = jnp.where(even, to_right, to_left)
    second_ref[...] = jnp.where(even, to_left, to_right)


def group_kernel(nodes, parity, local_ref, got_first, got_second, c_ref, nb_ref, sr, cs, out_ref):
    nc = nodes.nc
    elements = local_ref.shape[-1]
    left, right = ghosts(parity, got_first, got_second)
    count = left.shape[-1]
    from_left = select_columns(left, nb_ref[0:1, :] - elements, count)
    from_right = select_columns(right, nb_ref[1:2, :] - (elements + count), count)
    low = iota((8, elements), 0) < nodes.pc**2
    both = jnp.where(low, from_left, from_right)
    spread = nodes.face_spread(sr[...])[:, :8]
    scale = 1.0 / c_ref[...]
    total = (local_ref[:nc, :] + PENALTY * exact(spread, both)) * scale
    smoother = nodes.coarse_coarse(cs[...])
    out_ref[:nc, :] = exact(smoother, total)
    out_ref[nc:, :] = exact(smoother, local_ref[nc:, :])


def end_kernel(nodes, group, every_ref, x_ref, cs, trt, srt, out_ref):
    nc, n = nodes.nc, nodes.n
    transfer = COARSE_UPWIND * nodes.coarse_coarse(cs[...])
    mine = group[0]
    peers = every_ref.shape[0] // (2 * nc)
    state = jnp.zeros((nc, x_ref.shape[-1]), F32)
    for g in range(peers):
        at = 2 * nc * g
        after = exact(transfer, state) + every_ref[at : at + nc, :]
        if g:
            after = after + every_ref[at - nc : at, :]
        state = jnp.where(g <= mine, after, state)
    lifted = product(pieces(nodes.prolonged(trt[...], srt[...])), pieces(state))
    for s in range(x_ref.shape[0] // n):
        here = slice(s * n, (s + 1) * n)
        out_ref[here, :] = x_ref[here, :] + lifted


def call(kernel, nodes, outs, scratch=(), scalars=1):
    smem = [pl.BlockSpec(memory_space=pltpu.SMEM)] * scalars

    def run(*args):
        in_specs = smem + [pl.BlockSpec(memory_space=pltpu.VMEM)] * (len(args) - scalars)
        return pl.pallas_call(
            functools.partial(kernel, nodes),
            out_shape=[jax.ShapeDtypeStruct(shape, F32) for shape in outs],
            in_specs=in_specs,
            out_specs=[pl.BlockSpec(memory_space=pltpu.VMEM)] * len(outs),
            scratch_shapes=[pltpu.VMEM(shape, F32) for shape in scratch],
            compiler_params=pltpu.CompilerParams(vmem_limit_bytes=VMEM_BYTES),
            name=kernel.__name__,
        )(*args)

    return run


def swapped(first, second):
    peers = lax.axis_size("space")
    pairs = [[], []]
    for i in range(peers - 1):
        pairs[i % 2] += [(i, i + 1), (i + 1, i)]
    return [lax.ppermute(v, "space", q) for v, q in zip((first, second), pairs)]


def handed_on(last):
    peers = lax.axis_size("slab")
    return [lax.ppermute(last, "slab", [(i, i + 1) for i in range(k, peers - 1, 2)]) for k in (0, 1)]


def body(
    forcing, coefficient, neighbours, halo_faces, time_block, space_block, stiffness, time_restrict, space_restrict,
    coarse_smoother,
):
    slabs, q, p = forcing.shape[:3]
    elements = forcing.shape[-1]
    nodes = Nodes(q, p, space_restrict.shape[0])
    rows = slabs * nodes.n
    count = halo_faces.shape[-1]
    f = forcing.reshape(rows, elements)
    c = coefficient.reshape(1, elements)
    parity = (lax.axis_index("space") % 2).astype(jnp.int32).reshape(1)
    group = lax.axis_index("slab").astype(jnp.int32).reshape(1)
    field = (rows, elements)
    face = (rows // p, count)
    plane = (p**3, elements)
    nc = nodes.nc
    x1, first, second, last, rf = call(start_kernel, nodes, (field, face, face, plane, (nc, elements)))(
        parity, f, c, halo_faces, time_block, space_block, time_restrict, space_restrict
    )
    x = x1
    for sweep in range(SWEEPS - 1):
        got = swapped(first, second) + handed_on(last)
        (base,) = call(local_kernel, nodes, (field,), (field, (elements // 128, rows, 128)), 0)(
            x, x1, c, neighbours, time_block, space_block, stiffness
        )
        if sweep < SWEEPS - 2:
            x, first, second, last = call(finish_kernel, nodes, (field, face, face, plane), (field,))(
                parity, base, *got, c, neighbours, halo_faces, time_block, space_block
            )
        else:
            x, first, second, local = call(
                coarse_kernel, nodes, (field, (8, count), (8, count), (2 * nc, elements)), (field,)
            )(
                parity, base, *got, c, neighbours, halo_faces, rf, time_block, space_block, stiffness,
                time_restrict, space_restrict,
            )
    got = swapped(first, second)
    (mine,) = call(group_kernel, nodes, ((2 * nc, elements),))(
        parity, local, *got, c, neighbours, space_restrict, coarse_smoother
    )
    every = lax.all_gather(mine, "slab", axis=0, tiled=True)
    (out,) = call(end_kernel, nodes, (field,))(
        group, every, x, coarse_smoother, time_restrict.T, space_restrict.T
    )
    return out.reshape(forcing.shape)


def solution(mesh):
    in_specs = (
        P("slab", None, None, None, None, "space"),
        P("space"),
        P(None, "space"),
        P(None, "space"),
        P(),
        P(),
        P(),
        P(),
        P(),
        P(),
    )
    out_specs = P("slab", None, None, None, None, "space")
    return jax.shard_map(body, mesh=mesh, in_specs=in_specs, out_specs=out_specs, check_vma=False)
```

```python
import functools

import jax
import jax.numpy as jnp
from jax import lax
from jax.experimental import pallas as pl
from jax.experimental.pallas import tpu as pltpu
from jax.sharding import PartitionSpec as P

SWEEPS = 3
PENALTY = 0.3
UPWIND = 0.5
COARSE_UPWIND = 0.6
F32 = jnp.float32
BF16 = jnp.bfloat16
VMEM_BYTES = 28 * 1024 * 1024


def exact(a, b):
    return jnp.dot(a, b, precision=lax.Precision.HIGHEST, preferred_element_type=F32)


def iota(shape, dim):
    return lax.broadcasted_iota(jnp.int32, shape, dim)


def quotient(v, k):
    if k & (k - 1) == 0:
        return v >> (k.bit_length() - 1)
    return v // k


def digit(v, k, n):
    return quotient(v, k) & (n - 1) if n & (n - 1) == 0 else quotient(v, k) % n


def scalars(ref):
    return [[ref[i, j] for j in range(ref.shape[1])] for i in range(ref.shape[0])]


def two_minus(small):
    return [[(2.0 if i == j else 0.0) - v for j, v in enumerate(row)] for i, row in enumerate(small)]


def transposed(small):
    return [list(row) for row in zip(*small)]


def pick(at, values):
    out = jnp.full(at.shape, values[-1], F32)
    for k in range(len(values) - 2, -1, -1):
        out = jnp.where(at == k, values[k], out)
    return out


def combine(left, rows):
    outs = []
    for line in left:
        total = line[0] * rows[0]
        for k in range(1, len(rows)):
            total = total + line[k] * rows[k]
        outs.append(total)
    return outs


def row_select(vectors, which, masks):
    columns = vectors[0].shape[-1]
    distinct = sorted(set(which))
    out = jnp.broadcast_to(vectors[distinct[0]], (8, columns))
    for v in distinct[1:]:
        here = tuple(i for i in range(8) if which[i] == v)
        if (here, columns) not in masks:
            sub = iota((8, columns), 0)
            mask = sub == here[0]
            for i in here[1:]:
                mask = jnp.logical_or(mask, sub == i)
            masks[here, columns] = mask
        out = jnp.where(masks[here, columns], vectors[v], out)
    return out


class Nodes:
    def __init__(self, q, p, pc):
        self.q, self.p, self.pc = q, p, pc
        self.n = q * p**3
        self.nc = pc**3
        self.nf = 6 * pc**2
        self.masks = {}

    def fresh(self):
        return Nodes(self.q, self.p, self.pc)

    def fine(self, d, r):
        return quotient(r, self.p**3) if d == 0 else digit(r, self.p ** (3 - d), self.p)

    def coarse(self, d, r):
        return digit(r, self.pc ** (3 - d), self.pc)

    def bit(self, d, face, r):
        pc = self.pc
        if d == 1:
            return digit(r, pc, pc)
        if d == 3:
            return digit(r, 1, pc)
        return jnp.where(face < 2, digit(r, pc, pc), digit(r, 1, pc))

    def over_fine(self, small, d):
        at = self.fine(d, iota((1, self.n), 1))
        return [pick(at, line) for line in small]

    def over_coarse(self, small, d):
        at = self.coarse(d, iota((1, self.nc), 1))
        return [pick(at, line) for line in small]

    def rows_of(self, count, factors):
        parts = []
        for g in range(0, count, 8):
            total = None
            for vectors, row_digit in factors:
                term = row_select(vectors, [row_digit(g + i) for i in range(8)], self.masks)
                total = term if total is None else total * term
            parts.append(total)
        return jnp.concatenate(parts, axis=0) if len(parts) > 1 else parts[0]

    def fine_rows(self, time, x, y, z):
        return self.rows_of(
            self.n, [(v, functools.partial(self.fine, d)) for d, v in enumerate((time, x, y, z))]
        )

    def coarse_rows(self, time, x, y, z):
        return self.rows_of(
            self.nc,
            [(time, lambda r: 0)] + [(v, functools.partial(self.coarse, d)) for d, v in ((1, x), (2, y), (3, z))],
        )

    def kron(self, time, x, y, z):
        return self.fine_rows(*(self.over_fine(v, d) for d, v in enumerate((time, x, y, z))))

    def restricted(self, time, space):
        return self.coarse_rows(*(self.over_fine(v, d) for d, v in enumerate((time, space, space, space))))

    def prolonged(self, time, space):
        ones = jnp.ones((1, self.nc), F32)
        return self.fine_rows(
            [ones * v for v in time[0]], *(self.over_coarse(transposed(space), d) for d in (1, 2, 3))
        )

    def coarse_coarse(self, small):
        ones = [jnp.ones((1, self.nc), F32)]
        return self.coarse_rows(ones, *(self.over_coarse(small, d) for d in (1, 2, 3)))

    def face_traces(self, time, space):
        four, pc, p = self.pc**2, self.pc, self.p
        factors = [(self.over_fine(time, 0), lambda r: 0)]
        for d in (1, 2, 3):
            at = self.fine(d, iota((1, self.n), 1))
            vectors = self.over_fine(space, d)
            vectors = vectors + [(at == node).astype(F32) for node in (p - 1, 0)]

            def row_digit(r, d=d):
                face, high, low = r // four, r // pc % pc, r % pc
                if face // 2 == d - 1:
                    return pc + face % 2
                return high if d == 1 or (d == 2 and face < 2) else low

            factors.append((vectors, row_digit))
        return self.rows_of(self.nf, factors)

    def face_spread(self, space):
        col = iota((1, self.nf), 1)
        face = quotient(col, self.pc**2)
        factors = []
        for d in (1, 2, 3):
            vectors = []
            for i in range(self.pc):
                normal = jnp.where(digit(face, 1, 2) == 0, space[i][0], space[i][self.p - 1])
                tangential = (self.bit(d, face, col) == i).astype(F32)
                vectors.append(jnp.where(quotient(face, 2) == d - 1, normal, tangential))
            factors.append((vectors, functools.partial(self.coarse, d)))
        return self.rows_of(self.nc, factors)


def pieces(v):
    high = v.astype(BF16)
    return high, (v - high.astype(F32)).astype(BF16)


def bdot(a, b):
    return jnp.dot(a, b, preferred_element_type=F32)


def product(matrix, values):
    mh, ml = matrix
    vh, vl = values
    return bdot(mh, vh) + (bdot(mh, vl) + bdot(ml, vh))


def select_columns(values, indices, count):
    rows = values.shape[0]
    high, low = pieces(values)
    chosen = (iota((count, indices.shape[-1]), 0) == indices).astype(F32).astype(BF16)
    both = bdot(jnp.concatenate([high, low], axis=0), chosen)
    return both[:rows] + both[rows:]


def lower_half(shape):
    return iota(shape, 0) < 4


def trace_rows(ref, rows, face, p):
    d, node = face // 2, face % 2 * (p - 1)
    if d == 0:
        step = p * p
        return jnp.concatenate(
            [ref[r + node * step : r + (node + 1) * step, :] for r in range(0, rows, p * step)], axis=0
        )
    if d == 1:
        parts = []
        at = node * p // 8 * 8
        for r in range(0, rows, 2 * p * p):
            first = ref[r + at : r + at + 8, :]
            second = ref[r + p * p + at : r + p * p + at + 8, :]
            low = lower_half(first.shape)
            if node == 0:
                parts.append(jnp.where(low, first, pltpu.roll(second, 4, 0)))
            else:
                parts.append(jnp.where(low, pltpu.roll(first, 4, 0), second))
        return jnp.concatenate(parts, axis=0)
    raise ValueError(face)


def to_tiles(tiles_ref, ref):
    for k in range(tiles_ref.shape[0]):
        tiles_ref[k] = ref[:, 128 * k : 128 * k + 128]


def z_trace_rows(tiles_ref, rows, face, p):
    node = face % 2 * (p - 1)
    parts = [tiles_ref[k, pl.ds(node, rows // p, stride=p), :] for k in range(tiles_ref.shape[0])]
    return jnp.concatenate(parts, axis=1)


def z_put_rows(tiles_ref, values, rows, face, p):
    node = face % 2 * (p - 1)
    for k in range(tiles_ref.shape[0]):
        tiles_ref[k, pl.ds(node, rows // p, stride=p), :] = values[:, 128 * k : 128 * k + 128]


def add_rows(ref, values, rows, face, p):
    d, node = face // 2, face % 2 * (p - 1)
    if d == 0:
        step = p * p
        for i, r in enumerate(range(0, rows, p * step)):
            at = r + node * step
            ref[at : at + step, :] += values[i * step : (i + 1) * step]
    elif d == 1:
        at = node * p // 8 * 8
        for i, r in enumerate(range(0, rows, 2 * p * p)):
            eight = values[8 * i : 8 * i + 8]
            turned = pltpu.roll(eight, 4, 0)
            low = lower_half(eight.shape)
            if node == 0:
                first, second = jnp.where(low, eight, 0.0), jnp.where(low, turned, 0.0)
            else:
                first, second = jnp.where(low, 0.0, turned), jnp.where(low, 0.0, eight)
            ref[r + at : r + at + 8, :] += first
            ref[r + p * p + at : r + p * p + at + 8, :] += second


def last_time(nodes):
    return (nodes.q - 1) * nodes.p**3


def pack(x_ref, halo_ref, parity_ref, first_ref, second_ref, rows, p):
    elements = x_ref.shape[-1]
    to_left = select_columns(trace_rows(x_ref, rows, 0, p), halo_ref[0:1, :], elements)
    to_right = select_columns(trace_rows(x_ref, rows, 1, p), halo_ref[1:2, :], elements)
    even = parity_ref[0] == 0
    first_ref[...] = jnp.where(even, to_right, to_left)
    second_ref[...] = jnp.where(even, to_left, to_right)


def inverse_of(nodes, tb, sb):
    ti, si = two_minus(scalars(tb)), two_minus(scalars(sb))
    return pieces(nodes.kron(ti, si, si, si))


def from_halves(ref, row, p):
    tiles = []
    for k in range(0, ref.shape[1], 8):
        first, second = ref[row, k : k + 8, :], ref[row + 1, k : k + 8, :]
        low = lower_half(first.shape)
        tiles.append(jnp.where(low, first, pltpu.roll(second, 4, 0)))
        tiles.append(jnp.where(low, pltpu.roll(first, 4, 0), second))
    return jnp.concatenate(tiles, axis=1)


def to_halves(ref, row, values):
    for k in range(0, ref.shape[1], 8):
        at = 32 * k
        first, second = values[:, at : at + 128], values[:, at + 128 : at + 256]
        low = lower_half(first.shape)
        ref[row, k : k + 8, :] = jnp.where(low, first, pltpu.roll(second, 4, 0))
        ref[row + 1, k : k + 8, :] = jnp.where(low, pltpu.roll(first, 4, 0), second)


def start_kernel(nodes, parity, tb, sb, tr, sr, f_ref, c_ref, halo_ref, x_ref, first_ref, second_ref, last_ref, rf_ref):
    nodes = nodes.fresh()
    n, p = nodes.n, nodes.p
    rows = x_ref.shape[0]
    inverse = inverse_of(nodes, tb, sb)
    scale = 1.0 / c_ref[...]
    total = 0.0
    for s in range(rows // n):
        f = jnp.concatenate([from_halves(f_ref, (s * n + r) // p, p) for r in range(0, n, 8)], axis=0)
        total = total + f
        x_ref[s * n : (s + 1) * n, :] = product(inverse, pieces(f)) * scale
    pack(x_ref, halo_ref, parity, first_ref, second_ref, rows, p)
    at = rows - n + last_time(nodes)
    last_ref[...] = x_ref[at:rows, :]
    rf_ref[...] = product(pieces(nodes.restricted(scalars(tr), scalars(sr))), pieces(total))


def local_kernel(nodes, tb, sb, st, x_ref, x1_ref, c_ref, nb_ref, out_ref, g_ref, tiles_ref):
    nodes = nodes.fresh()
    n, p = nodes.n, nodes.p
    rows, elements = x_ref.shape
    plane = p**3
    t, b, d = scalars(tb), scalars(sb), scalars(st)
    ti, si = two_minus(t), two_minus(b)
    et = nodes.over_fine(ti, 0)
    es = [nodes.over_fine(si, k) for k in (1, 2, 3)]
    ed = [combine(si, nodes.over_fine(d, k)) for k in (1, 2, 3)]
    eb = [combine(si, nodes.over_fine(b, k)) for k in (1, 2, 3)]
    inverse = pieces(nodes.fine_rows(et, *es))
    unit = (iota((n, n), 0) == iota((n, n), 1)).astype(F32)
    keep = pieces(unit - nodes.fine_rows(combine(ti, nodes.over_fine(t, 0)), *eb))
    drift = nodes.fine_rows(et, ed[0], es[1], es[2]) + nodes.fine_rows(et, es[0], ed[1], es[2])
    drift = pieces(-(drift + nodes.fine_rows(et, es[0], es[1], ed[2])))
    c = c_ref[...]
    scale = 1.0 / c
    g_ref[...] = jnp.zeros_like(g_ref)
    for s in range(1, rows // n):
        before = (s - 1) * n + last_time(nodes)
        g_ref[s * n : s * n + plane, :] = UPWIND * c * x_ref[before : before + plane, :]
    to_tiles(tiles_ref, x_ref)
    z_values = [z_trace_rows(tiles_ref, rows, face ^ 1, p) for face in (4, 5)]
    tiles_ref[...] = jnp.zeros_like(tiles_ref)
    for face in range(6):
        values = trace_rows(x_ref, rows, face ^ 1, p) if face < 4 else z_values[face - 4]
        coupled = PENALTY * select_columns(values, nb_ref[face : face + 1, :], elements)
        if face < 4:
            add_rows(g_ref, coupled, rows, face, p)
        else:
            z_put_rows(tiles_ref, coupled, rows, face, p)
    for k in range(tiles_ref.shape[0]):
        g_ref[:, 128 * k : 128 * k + 128] += tiles_ref[k]
    for s in range(rows // n):
        here = slice(s * n, (s + 1) * n)
        x = pieces(x_ref[here, :])
        turned = product(drift, x) + product(inverse, pieces(g_ref[here, :]))
        out_ref[here, :] = x1_ref[here, :] + product(keep, x) + scale * turned


def ghosts(parity_ref, got_first_ref, got_second_ref):
    even = parity_ref[0] == 0
    first, second = got_first_ref[...], got_second_ref[...]
    return jnp.where(even, second, first), jnp.where(even, first, second)


def finish(nodes, parity, tb, sb, base_ref, got_first, got_second, prev_a, prev_b, c_ref, nb_ref, x_ref, g_ref):
    n, p = nodes.n, nodes.p
    rows, elements = base_ref.shape
    inverse = inverse_of(nodes, tb, sb)
    c = c_ref[...]
    scale = 1.0 / c
    left, right = ghosts(parity, got_first, got_second)
    count = left.shape[-1]
    g_ref[...] = jnp.zeros_like(g_ref)
    g_ref[: p**3, :] = UPWIND * c * (prev_a[...] + prev_b[...])
    add_rows(g_ref, PENALTY * select_columns(left, nb_ref[0:1, :] - elements, count), rows, 0, p)
    add_rows(g_ref, PENALTY * select_columns(right, nb_ref[1:2, :] - (elements + count), count), rows, 1, p)
    for s in range(rows // n):
        here = slice(s * n, (s + 1) * n)
        x_ref[here, :] = base_ref[here, :] + scale * product(inverse, pieces(g_ref[here, :]))


def finish_kernel(
    nodes, parity, tb, sb, base_ref, got_first, got_second, prev_a, prev_b, c_ref, nb_ref, halo_ref,
    x_ref, first_ref, second_ref, last_ref, g_ref,
):
    nodes = nodes.fresh()
    finish(nodes, parity, tb, sb, base_ref, got_first, got_second, prev_a, prev_b, c_ref, nb_ref, x_ref, g_ref)
    rows = base_ref.shape[0]
    pack(x_ref, halo_ref, parity, first_ref, second_ref, rows, nodes.p)
    last_ref[...] = x_ref[rows - nodes.n + last_time(nodes) : rows, :]


def coarse_kernel(
    nodes, parity, tb, sb, st, tr, sr, base_ref, got_first, got_second, prev_a, prev_b, c_ref, nb_ref, halo_ref, rf_ref,
    x_ref, first_ref, second_ref, local_ref, g_ref,
):
    nodes = nodes.fresh()
    finish(nodes, parity, tb, sb, base_ref, got_first, got_second, prev_a, prev_b, c_ref, nb_ref, x_ref, g_ref)
    n, p, nc = nodes.n, nodes.p, nodes.nc
    rows, elements = x_ref.shape
    t, s = scalars(tr), scalars(sr)
    et = nodes.over_fine(t, 0)
    es = [nodes.over_fine(s, k) for k in (1, 2, 3)]
    ed = [combine(s, nodes.over_fine(scalars(st), k)) for k in (1, 2, 3)]
    eb = [combine(s, nodes.over_fine(scalars(sb), k)) for k in (1, 2, 3)]
    block = nodes.coarse_rows(combine(t, nodes.over_fine(scalars(tb), 0)), *eb)
    stiff = nodes.coarse_rows(et, ed[0], es[1], es[2]) + nodes.coarse_rows(et, es[0], ed[1], es[2])
    stiff = stiff + nodes.coarse_rows(et, es[0], es[1], ed[2])
    faces = nodes.face_traces(t, s)
    stacked = pieces(jnp.concatenate([block, stiff, faces], axis=0))
    total = x_ref[:n, :]
    before = 0.0
    for k in range(1, rows // n):
        total = total + x_ref[k * n : (k + 1) * n, :]
        at = (k - 1) * n + last_time(nodes)
        before = before + x_ref[at : at + p**3, :]
    applied = product(stacked, pieces(total))
    first_node = pieces(nodes.coarse_rows(et, *es)[:, : p**3])
    c = c_ref[...]
    local = rf_ref[...] - c * applied[:nc] - applied[nc : 2 * nc]
    local = local + (UPWIND * c) * product(first_node, pieces(before))
    traces = applied[2 * nc :]
    high, low = pieces(traces)
    both = jnp.concatenate([high, low], axis=0)
    four = nodes.pc**2
    row = iota((nodes.nf, elements), 0) // four
    coupled = 0.0
    for face in range(6):
        chosen = (iota((elements, elements), 0) == nb_ref[face : face + 1, :]).astype(F32).astype(BF16)
        got = bdot(both, chosen)
        coupled = coupled + jnp.where(row == face, got[: nodes.nf] + got[nodes.nf :], 0.0)
    spread = nodes.face_spread(s)
    local_ref[:nc, :] = local + PENALTY * exact(spread, coupled)
    end = x_ref[rows - n + last_time(nodes) : rows, :]
    local_ref[nc:, :] = UPWIND * product(first_node, pieces(end))
    to_left = select_columns(traces[:8], halo_ref[0:1, :], elements)
    to_right = select_columns(traces[:8], halo_ref[1:2, :], elements)
    even = parity[0] == 0
    first_ref[...] = jnp.where(even, to_right, to_left)
    second_ref[...] = jnp.where(even, to_left, to_right)


def group_kernel(nodes, parity, sr, cs, local_ref, got_first, got_second, c_ref, nb_ref, out_ref):
    nodes = nodes.fresh()
    nc = nodes.nc
    elements = local_ref.shape[-1]
    left, right = ghosts(parity, got_first, got_second)
    count = left.shape[-1]
    from_left = select_columns(left, nb_ref[0:1, :] - elements, count)
    from_right = select_columns(right, nb_ref[1:2, :] - (elements + count), count)
    low = iota((8, elements), 0) < nodes.pc**2
    both = jnp.where(low, from_left, from_right)
    spread = nodes.face_spread(scalars(sr))[:, :8]
    scale = 1.0 / c_ref[...]
    total = (local_ref[:nc, :] + PENALTY * exact(spread, both)) * scale
    smoother = nodes.coarse_coarse(scalars(cs))
    out_ref[:nc, :] = exact(smoother, total)
    out_ref[nc:, :] = exact(smoother, local_ref[nc:, :])


def end_kernel(nodes, group, cs, tr, sr, every_ref, x_ref, out_ref):
    nodes = nodes.fresh()
    nc, n, p = nodes.nc, nodes.n, nodes.p
    transfer = COARSE_UPWIND * nodes.coarse_coarse(scalars(cs))
    mine = group[0]
    peers = every_ref.shape[0] // (2 * nc)
    state = jnp.zeros((nc, x_ref.shape[-1]), F32)
    for g in range(peers):
        at = 2 * nc * g
        after = exact(transfer, state) + every_ref[at : at + nc, :]
        if g:
            after = after + every_ref[at - nc : at, :]
        state = jnp.where(g <= mine, after, state)
    lifted = product(pieces(nodes.prolonged(scalars(tr), scalars(sr))), pieces(state))
    for r in range(0, x_ref.shape[0], 8):
        to_halves(out_ref, r // p, x_ref[r : r + 8, :] + lifted[r % n : r % n + 8, :])


def call(kernel, nodes, outs, small, scratch=()):
    def run(*args):
        in_specs = [pl.BlockSpec(memory_space=pltpu.SMEM)] * len(small)
        in_specs += [pl.BlockSpec(memory_space=pltpu.VMEM)] * len(args)
        return pl.pallas_call(
            functools.partial(kernel, nodes),
            out_shape=[jax.ShapeDtypeStruct(shape, F32) for shape in outs],
            in_specs=in_specs,
            out_specs=[pl.BlockSpec(memory_space=pltpu.VMEM)] * len(outs),
            scratch_shapes=[pltpu.VMEM(shape, F32) for shape in scratch],
            compiler_params=pltpu.CompilerParams(vmem_limit_bytes=VMEM_BYTES),
            name=kernel.__name__,
        )(*small, *args)

    return run


def swapped(first, second):
    peers = lax.axis_size("space")
    pairs = [[], []]
    for i in range(peers - 1):
        pairs[i % 2] += [(i, i + 1), (i + 1, i)]
    return [lax.ppermute(v, "space", q) for v, q in zip((first, second), pairs)]


def handed_on(last):
    peers = lax.axis_size("slab")
    return [lax.ppermute(last, "slab", [(i, i + 1) for i in range(k, peers - 1, 2)]) for k in (0, 1)]


def body(
    forcing, coefficient, neighbours, halo_faces, time_block, space_block, stiffness, time_restrict, space_restrict,
    coarse_smoother,
):
    slabs, q, p = forcing.shape[:3]
    elements = forcing.shape[-1]
    nodes = Nodes(q, p, space_restrict.shape[0])
    rows = slabs * nodes.n
    count = halo_faces.shape[-1]
    tiles = elements // 128
    halves = (rows // p, tiles * p, 128)
    f = forcing.reshape(rows // p, p, tiles, 128).transpose(0, 2, 1, 3).reshape(halves)
    c = coefficient.reshape(1, elements)
    parity = (lax.axis_index("space") % 2).astype(jnp.int32).reshape(1)
    group = lax.axis_index("slab").astype(jnp.int32).reshape(1)
    field = (rows, elements)
    face = (rows // p, count)
    plane = (p**3, elements)
    nc = nodes.nc
    tb, sb, st, tr, sr, cs = time_block, space_block, stiffness, time_restrict, space_restrict, coarse_smoother
    x1, first, second, last, rf = call(
        start_kernel, nodes, (field, face, face, plane, (nc, elements)), (parity, tb, sb, tr, sr)
    )(f, c, halo_faces)
    x = x1
    for sweep in range(SWEEPS - 1):
        got = swapped(first, second) + handed_on(last)
        (base,) = call(local_kernel, nodes, (field,), (tb, sb, st), (field, (tiles, rows, 128)))(x, x1, c, neighbours)
        if sweep < SWEEPS - 2:
            x, first, second, last = call(
                finish_kernel, nodes, (field, face, face, plane), (parity, tb, sb), (field,)
            )(base, *got, c, neighbours, halo_faces)
        else:
            x, first, second, local = call(
                coarse_kernel, nodes, (field, (8, count), (8, count), (2 * nc, elements)),
                (parity, tb, sb, st, tr, sr), (field,),
            )(base, *got, c, neighbours, halo_faces, rf)
    got = swapped(first, second)
    (mine,) = call(group_kernel, nodes, ((2 * nc, elements),), (parity, sr, cs))(local, *got, c, neighbours)
    every = lax.all_gather(mine, "slab", axis=0, tiled=True)
    (out,) = call(end_kernel, nodes, (halves,), (group, cs, tr, sr))(every, x)
    out = out.reshape(rows // p, tiles, p, 128).transpose(0, 2, 1, 3)
    return out.reshape(forcing.shape)


def solution(mesh):
    in_specs = (
        P("slab", None, None, None, None, "space"),
        P("space"),
        P(None, "space"),
        P(None, "space"),
        P(),
        P(),
        P(),
        P(),
        P(),
        P(),
    )
    out_specs = P("slab", None, None, None, None, "space")
    return jax.shard_map(body, mesh=mesh, in_specs=in_specs, out_specs=out_specs, check_vma=False)
```

```python
import functools

import jax
import jax.numpy as jnp
from jax import lax
from jax.experimental import pallas as pl
from jax.experimental.pallas import tpu as pltpu
from jax.sharding import PartitionSpec as P

SWEEPS = 3
PENALTY = 0.3
UPWIND = 0.5
COARSE_UPWIND = 0.6
F32 = jnp.float32
BF16 = jnp.bfloat16
VMEM_BYTES = 28 * 1024 * 1024


def iota(shape, dim):
    return lax.broadcasted_iota(jnp.int32, shape, dim)


def quotient(v, k):
    if k & (k - 1) == 0:
        return v >> (k.bit_length() - 1)
    return v // k


def digit(v, k, n):
    return quotient(v, k) & (n - 1) if n & (n - 1) == 0 else quotient(v, k) % n


def scalars(ref):
    return [[ref[i, j] for j in range(ref.shape[1])] for i in range(ref.shape[0])]


def two_minus(small):
    return [[(2.0 if i == j else 0.0) - v for j, v in enumerate(row)] for i, row in enumerate(small)]


def transposed(small):
    return [list(row) for row in zip(*small)]


def small_product(a, b):
    return [[sum(a[i][k] * b[k][j] for k in range(len(b))) for j in range(len(b[0]))] for i in range(len(a))]


def pick(at, values):
    out = jnp.zeros(at.shape, F32) + values[-1]
    for k in range(len(values) - 2, -1, -1):
        out = jnp.where(at == k, values[k], out)
    return out


def combine(left, rows):
    outs = []
    for line in left:
        total = line[0] * rows[0]
        for k in range(1, len(rows)):
            total = total + line[k] * rows[k]
        outs.append(total)
    return outs


def row_select(vectors, which, masks):
    columns = vectors[0].shape[-1]
    distinct = sorted(set(which))
    out = jnp.broadcast_to(vectors[distinct[0]], (8, columns))
    for v in distinct[1:]:
        here = tuple(i for i in range(8) if which[i] == v)
        if (here, columns) not in masks:
            sub = iota((8, columns), 0)
            mask = sub == here[0]
            for i in here[1:]:
                mask = jnp.logical_or(mask, sub == i)
            masks[here, columns] = mask
        out = jnp.where(masks[here, columns], vectors[v], out)
    return out


class Nodes:
    def __init__(self, q, p, pc):
        self.q, self.p, self.pc = q, p, pc
        self.n = q * p**3
        self.nc = pc**3
        self.nf = 6 * pc**2
        self.masks = {}

    def fresh(self):
        return Nodes(self.q, self.p, self.pc)

    def fine(self, d, r):
        return quotient(r, self.p**3) if d == 0 else digit(r, self.p ** (3 - d), self.p)

    def coarse(self, d, r):
        return digit(r, self.pc ** (3 - d), self.pc)

    def bit(self, d, face, r):
        pc = self.pc
        if d == 1:
            return digit(r, pc, pc)
        if d == 3:
            return digit(r, 1, pc)
        return jnp.where(face < 2, digit(r, pc, pc), digit(r, 1, pc))

    def over_fine(self, small, d):
        at = self.fine(d, iota((1, self.n), 1))
        return [pick(at, line) for line in small]

    def rows_of(self, count, factors):
        parts = []
        for g in range(0, count, 8):
            total = None
            for vectors, row_digit in factors:
                term = row_select(vectors, [row_digit(g + i) for i in range(8)], self.masks)
                total = term if total is None else total * term
            parts.append(total)
        return jnp.concatenate(parts, axis=0) if len(parts) > 1 else parts[0]

    def fine_rows(self, time, x, y, z):
        return self.rows_of(
            self.n, [(v, functools.partial(self.fine, d)) for d, v in enumerate((time, x, y, z))]
        )

    def coarse_rows(self, time, x, y, z):
        return self.rows_of(
            self.nc,
            [(time, lambda r: 0)] + [(v, functools.partial(self.coarse, d)) for d, v in ((1, x), (2, y), (3, z))],
        )

    def kron(self, time, x, y, z):
        return self.fine_rows(*(self.over_fine(v, d) for d, v in enumerate((time, x, y, z))))

    def restricted(self, time, space):
        return self.coarse_rows(*(self.over_fine(v, d) for d, v in enumerate((time, space, space, space))))

    def lifted(self, time, space, smoother, mine, sources):
        width = 2 * self.nc
        col = iota((1, width * len(sources)), 1)
        block = quotient(col, width)
        owner = jnp.zeros_like(col) + sources[0]
        for k in range(1, len(sources)):
            owner = jnp.where(block == k, sources[k], owner)
        steps = mine - owner - digit(col, self.nc, 2)
        power, decay, powers, decays = smoother, 1.0, [], []
        for _ in sources:
            powers.append(small_product(transposed(space), power))
            decays.append(decay)
            power, decay = small_product(power, smoother), decay * COARSE_UPWIND
        weight = jnp.where(steps < 0, 0.0, pick(steps, decays))
        factors = [[weight * v for v in time[0]]]
        for d in (1, 2, 3):
            at = self.coarse(d, col)
            factors.append(
                [pick(at, [pick(steps, [z[x][i] for z in powers]) for i in range(self.pc)]) for x in range(self.p)]
            )
        return self.fine_rows(*factors)

    def face_traces(self, time, space):
        four, pc, p = self.pc**2, self.pc, self.p
        factors = [(self.over_fine(time, 0), lambda r: 0)]
        for d in (1, 2, 3):
            at = self.fine(d, iota((1, self.n), 1))
            vectors = self.over_fine(space, d)
            vectors = vectors + [(at == node).astype(F32) for node in (p - 1, 0)]

            def row_digit(r, d=d):
                face, high, low = r // four, r // pc % pc, r % pc
                if face // 2 == d - 1:
                    return pc + face % 2
                return high if d == 1 or (d == 2 and face < 2) else low

            factors.append((vectors, row_digit))
        return self.rows_of(self.nf, factors)

    def face_spread(self, space):
        col = iota((1, self.nf), 1)
        face = quotient(col, self.pc**2)
        factors = []
        for d in (1, 2, 3):
            vectors = []
            for i in range(self.pc):
                normal = jnp.where(digit(face, 1, 2) == 0, space[i][0], space[i][self.p - 1])
                tangential = (self.bit(d, face, col) == i).astype(F32)
                vectors.append(jnp.where(quotient(face, 2) == d - 1, normal, tangential))
            factors.append((vectors, functools.partial(self.coarse, d)))
        return self.rows_of(self.nc, factors)


def pieces(v):
    high = v.astype(BF16)
    return high, (v - high.astype(F32)).astype(BF16)


def bdot(a, b):
    return jnp.dot(a, b, preferred_element_type=F32)


def product(matrix, values):
    mh, ml = matrix
    vh, vl = values
    return bdot(mh, vh) + (bdot(mh, vl) + bdot(ml, vh))


def lane_select(values, indices):
    outs = []
    for j in range(0, indices.shape[-1], 128):
        at = indices[:, j : j + 128]
        tile, lane = at >> 7, at & 127
        out = jnp.zeros(at.shape, F32)
        for k in range(values.shape[-1] // 128):
            got = jnp.take_along_axis(values[:, 128 * k : 128 * k + 128], lane, axis=1, mode="promise_in_bounds")
            out = jnp.where(tile == k, got, out)
        outs.append(out)
    return jnp.concatenate(outs, axis=1)


def select_columns(values, indices, count):
    rows = values.shape[0]
    high, low = pieces(values)
    chosen = (iota((count, indices.shape[-1]), 0) == indices).astype(F32).astype(BF16)
    both = bdot(jnp.concatenate([high, low], axis=0), chosen)
    return both[:rows] + both[rows:]


def lower_half(shape):
    return iota(shape, 0) < 4


def load(ref, start, stop):
    return jnp.concatenate([ref[k, start:stop, :] for k in range(ref.shape[0])], axis=1)


def store(ref, start, values):
    for k in range(ref.shape[0]):
        ref[k, start : start + values.shape[0], :] = values[:, 128 * k : 128 * k + 128]


def accumulate(ref, start, values):
    for k in range(ref.shape[0]):
        ref[k, start : start + values.shape[0], :] += values[:, 128 * k : 128 * k + 128]


def trace_rows(ref, face, p):
    rows = ref.shape[1]
    d, node = face // 2, face % 2 * (p - 1)
    if d == 0:
        step = p * p
        parts = [load(ref, r + node * step, r + (node + 1) * step) for r in range(0, rows, p * step)]
        return jnp.concatenate(parts, axis=0)
    if d == 1:
        parts = []
        at = node * p // 8 * 8
        for r in range(0, rows, 2 * p * p):
            first = load(ref, r + at, r + at + 8)
            second = load(ref, r + p * p + at, r + p * p + at + 8)
            low = lower_half(first.shape)
            if node == 0:
                parts.append(jnp.where(low, first, pltpu.roll(second, 4, 0)))
            else:
                parts.append(jnp.where(low, pltpu.roll(first, 4, 0), second))
        return jnp.concatenate(parts, axis=0)
    parts = [ref[k, pl.ds(node, rows // p, stride=p), :] for k in range(ref.shape[0])]
    return jnp.concatenate(parts, axis=1)


def add_rows(ref, values, face, p):
    rows = ref.shape[1]
    d, node = face // 2, face % 2 * (p - 1)
    if d == 0:
        step = p * p
        for i, r in enumerate(range(0, rows, p * step)):
            accumulate(ref, r + node * step, values[i * step : (i + 1) * step])
    elif d == 1:
        at = node * p // 8 * 8
        for i, r in enumerate(range(0, rows, 2 * p * p)):
            eight = values[8 * i : 8 * i + 8]
            turned = pltpu.roll(eight, 4, 0)
            low = lower_half(eight.shape)
            if node == 0:
                first, second = jnp.where(low, eight, 0.0), jnp.where(low, turned, 0.0)
            else:
                first, second = jnp.where(low, 0.0, turned), jnp.where(low, 0.0, eight)
            accumulate(ref, r + at, first)
            accumulate(ref, r + p * p + at, second)
    else:
        for k in range(ref.shape[0]):
            where = (k, pl.ds(node, rows // p, stride=p), slice(None))
            ref[where] = ref[where] + values[:, 128 * k : 128 * k + 128]


def from_halves(ref, row):
    tiles = []
    for k in range(0, ref.shape[1], 8):
        first, second = ref[row, k : k + 8, :], ref[row + 1, k : k + 8, :]
        low = lower_half(first.shape)
        tiles.append(jnp.where(low, first, pltpu.roll(second, 4, 0)))
        tiles.append(jnp.where(low, pltpu.roll(first, 4, 0), second))
    return jnp.concatenate(tiles, axis=1)


def to_halves(ref, row, values):
    for k in range(0, ref.shape[1], 8):
        at = 32 * k
        first, second = values[:, at : at + 128], values[:, at + 128 : at + 256]
        low = lower_half(first.shape)
        ref[row, k : k + 8, :] = jnp.where(low, first, pltpu.roll(second, 4, 0))
        ref[row + 1, k : k + 8, :] = jnp.where(low, pltpu.roll(first, 4, 0), second)


def keep_pieces(ref, matrix):
    high, low = pieces(matrix)
    ref[0] = high
    ref[1] = low


def both_pieces(ref):
    return ref[0], ref[1]


def last_time(nodes):
    return (nodes.q - 1) * nodes.p**3


def is_even():
    return lax.axis_index("space") % 2 == 0


def pack(x_ref, halo_ref, first_ref, second_ref, p):
    elements = x_ref.shape[0] * 128
    to_left = select_columns(trace_rows(x_ref, 0, p), halo_ref[0:1, :], elements)
    to_right = select_columns(trace_rows(x_ref, 1, p), halo_ref[1:2, :], elements)
    even = is_even()
    first_ref[...] = jnp.where(even, to_right, to_left)
    second_ref[...] = jnp.where(even, to_left, to_right)


def sources_of(mine, peers):
    if peers & (peers - 1) == 0:
        return [mine ^ k for k in range(peers)]
    return [mine - k for k in range(peers)]


def start_kernel(
    nodes, peers, f_hbm, c_hbm, nb_hbm, halo_hbm, tb_hbm, sb_hbm, st_hbm, tr_hbm, sr_hbm, cs_hbm,
    x_ref, first_ref, second_ref, last_ref, rf_ref, c_ref, nb_ref, halo_ref,
    inverse_ref, step_ref, coarse_ref, lift_ref, spread_ref, ends_ref,
    f_ref, tb, sb, st, tr, sr, cs, small_sem, table_sem, field_sem,
):
    nodes = nodes.fresh()
    n, p, nc = nodes.n, nodes.p, nodes.nc
    rows = x_ref.shape[1]
    small = [(tb_hbm, tb), (sb_hbm, sb), (st_hbm, st), (tr_hbm, tr), (sr_hbm, sr), (cs_hbm, cs)]
    tables = [(c_hbm, c_ref), (nb_hbm, nb_ref), (halo_hbm, halo_ref)]
    small = [pltpu.make_async_copy(a, b, small_sem.at[i]) for i, (a, b) in enumerate(small)]
    tables = [pltpu.make_async_copy(a, b, table_sem.at[i]) for i, (a, b) in enumerate(tables)]
    slabs = rows // n
    size = n // p
    fields = [
        pltpu.make_async_copy(f_hbm.at[pl.ds(s * size, size)], f_ref.at[pl.ds(s * size, size)], field_sem.at[s])
        for s in range(slabs)
    ]
    for copy in small + fields + tables:
        copy.start()
    for copy in small:
        copy.wait()
    t, b, d, tt, ss, w = (scalars(ref) for ref in (tb, sb, st, tr, sr, cs))
    ti, si = two_minus(t), two_minus(b)
    et = nodes.over_fine(ti, 0)
    es = [nodes.over_fine(si, k) for k in (1, 2, 3)]
    of_b = [nodes.over_fine(b, k) for k in (1, 2, 3)]
    of_d = [nodes.over_fine(d, k) for k in (1, 2, 3)]
    of_t = nodes.over_fine(t, 0)
    inverse = pieces(nodes.fine_rows(et, *es))
    inverse_ref[0], inverse_ref[1] = inverse
    unit = (iota((n, n), 0) == iota((n, n), 1)).astype(F32)
    keep = unit - nodes.fine_rows(combine(ti, of_t), *(combine(si, v) for v in of_b))
    ed = [combine(si, v) for v in of_d]
    drift = nodes.fine_rows(et, ed[0], es[1], es[2]) + nodes.fine_rows(et, es[0], ed[1], es[2])
    drift = -(drift + nodes.fine_rows(et, es[0], es[1], ed[2]))
    keep_pieces(step_ref, jnp.concatenate([keep, drift], axis=0))
    rt = nodes.over_fine(tt, 0)
    rs = [nodes.over_fine(ss, k) for k in (1, 2, 3)]
    rd = [combine(ss, v) for v in of_d]
    block = nodes.coarse_rows(combine(tt, of_t), *(combine(ss, v) for v in of_b))
    stiff = nodes.coarse_rows(rt, rd[0], rs[1], rs[2]) + nodes.coarse_rows(rt, rs[0], rd[1], rs[2])
    stiff = stiff + nodes.coarse_rows(rt, rs[0], rs[1], rd[2])
    restrict = nodes.coarse_rows(rt, *rs)
    keep_pieces(coarse_ref, jnp.concatenate([restrict, block, stiff, nodes.face_traces(tt, ss)], axis=0))
    mine = lax.axis_index("slab")
    keep_pieces(lift_ref, nodes.lifted(tt, ss, w, mine, sources_of(mine, peers)))
    spread_ref[...] = nodes.face_spread(ss)
    sub = iota((8, 128), 0)
    half = nodes.pc**2
    ends_ref[0] = jnp.where(sub < half, ss[0][0], ss[1][0])
    ends_ref[1] = jnp.where(sub < half, ss[0][p - 1], ss[1][p - 1])
    tables[0].wait()
    scale = 1.0 / c_ref[...]
    total = 0.0
    for s in range(slabs):
        fields[s].wait()
        f = jnp.concatenate([from_halves(f_ref, (s * n + r) // p) for r in range(0, n, 8)], axis=0)
        total = total + f
        store(x_ref, s * n, product(inverse, pieces(f)) * scale)
    tables[1].wait()
    tables[2].wait()
    pack(x_ref, halo_ref, first_ref, second_ref, p)
    last_ref[...] = load(x_ref, rows - n + last_time(nodes), rows)
    high, low = pieces(restrict)
    rf_ref[...] = product((high, low), pieces(total))


def local_kernel(nodes, x_ref, x1_ref, c_ref, nb_ref, step_ref, base_ref, g_ref):
    n, p = nodes.n, nodes.p
    rows = x_ref.shape[1]
    elements = x_ref.shape[0] * 128
    c = c_ref[...]
    scale = 1.0 / c
    g_ref[...] = jnp.zeros_like(g_ref)
    for s in range(1, rows // n):
        before = (s - 1) * n + last_time(nodes)
        store(g_ref, s * n, UPWIND * c * load(x_ref, before, before + p**3))
    step = both_pieces(step_ref)
    for face in range(6):
        values = trace_rows(x_ref, face ^ 1, p)
        add_rows(g_ref, PENALTY * select_columns(values, nb_ref[face : face + 1, :], elements), face, p)
    for s in range(rows // n):
        moved = product(step, pieces(load(x_ref, s * n, (s + 1) * n)))
        store(base_ref, s * n, load(x1_ref, s * n, (s + 1) * n) + moved[:n] + scale * moved[n:])


def finish(nodes, base_ref, g_ref, got_first, got_second, prev_a, prev_b, c_ref, nb_ref, inverse_ref, x_ref):
    n, p = nodes.n, nodes.p
    rows = base_ref.shape[1]
    elements = base_ref.shape[0] * 128
    inverse = both_pieces(inverse_ref)
    c = c_ref[...]
    scale = 1.0 / c
    even = is_even()
    first, second = got_first[...], got_second[...]
    left, right = jnp.where(even, second, first), jnp.where(even, first, second)
    count = left.shape[-1]
    left = PENALTY * select_columns(left, nb_ref[0:1, :] - elements, count)
    right = PENALTY * select_columns(right, nb_ref[1:2, :] - (elements + count), count)
    handed = (UPWIND * c) * (prev_a[...] + prev_b[...])
    step = p * p
    for s in range(rows // n):
        parts = []
        for time in range(nodes.q):
            at = (s * nodes.q + time) * step
            for x in range(p):
                start = s * n + time * p**3 + x * step
                part = load(g_ref, start, start + step)
                if x == 0:
                    part = part + left[at : at + step]
                if x == p - 1:
                    part = part + right[at : at + step]
                if s == 0 and time == 0:
                    part = part + handed[x * step : (x + 1) * step]
                parts.append(part)
        moved = product(inverse, pieces(jnp.concatenate(parts, axis=0)))
        store(x_ref, s * n, load(base_ref, s * n, (s + 1) * n) + scale * moved)


def finish_kernel(
    nodes, base_ref, g_ref, got_first, got_second, prev_a, prev_b, c_ref, nb_ref, inverse_ref, halo_ref,
    x_ref, first_ref, second_ref, last_ref,
):
    finish(nodes, base_ref, g_ref, got_first, got_second, prev_a, prev_b, c_ref, nb_ref, inverse_ref, x_ref)
    rows = base_ref.shape[1]
    pack(x_ref, halo_ref, first_ref, second_ref, nodes.p)
    last_ref[...] = load(x_ref, rows - nodes.n + last_time(nodes), rows)


def coarse_kernel(
    nodes, base_ref, g_ref, got_first, got_second, prev_a, prev_b, c_ref, nb_ref, inverse_ref, halo_ref,
    coarse_ref, spread_ref, rf_ref,
    x_ref, packed_ref, local_ref,
):
    finish(nodes, base_ref, g_ref, got_first, got_second, prev_a, prev_b, c_ref, nb_ref, inverse_ref, x_ref)
    n, p, nc = nodes.n, nodes.p, nodes.nc
    rows = x_ref.shape[1]
    elements = x_ref.shape[0] * 128
    half = nodes.pc**2
    high, low = both_pieces(coarse_ref)
    total = load(x_ref, 0, n)
    before = 0.0
    for k in range(1, rows // n):
        total = total + load(x_ref, k * n, (k + 1) * n)
        at = (k - 1) * n + last_time(nodes)
        before = before + load(x_ref, at, at + p**3)
    applied = product((high, low), pieces(total))[nc:]
    traces = applied[2 * nc :]
    halo = halo_ref[...]
    packed_ref[...] = lane_select(
        traces[:8], jnp.where(iota((8, halo.shape[-1]), 0) < half, halo[1:2, :], halo[0:1, :])
    )
    low_half = iota((8, elements), 0) < half
    coupled = [
        lane_select(
            traces[8 * k : 8 * k + 8],
            jnp.where(low_half, nb_ref[2 * k : 2 * k + 1, :], nb_ref[2 * k + 1 : 2 * k + 2, :]),
        )
        for k in range(3)
    ]
    c = c_ref[...]
    end = load(x_ref, rows - n + last_time(nodes), rows)
    plane = p**3
    moved = product((high[:, :plane], low[:, :plane]), pieces(jnp.concatenate([before, end], axis=1)))[:nc]
    local = rf_ref[...] - c * applied[:nc] - applied[nc : 2 * nc] + (UPWIND * c) * moved[:, :elements]
    spread = product(pieces(spread_ref[...]), pieces(jnp.concatenate(coupled, axis=0)))
    local_ref[:nc, :] = local + PENALTY * spread
    local_ref[nc:, :] = UPWIND * moved[:, elements:]


def group_kernel(nodes, local_ref, got_first, got_second, c_ref, nb_ref, ends_ref, out_ref):
    nc = nodes.nc
    elements = local_ref.shape[-1]
    half = nodes.pc**2
    first, second = got_first[...], got_second[...]
    count = first.shape[-1]
    even = is_even()
    left, right = jnp.where(even, second, first), jnp.where(even, first, second)
    both = jnp.where(iota((8, count), 0) < half, left, right)
    low = iota((8, elements), 0) < half
    at = jnp.where(low, nb_ref[0:1, :] - elements, nb_ref[1:2, :] - (elements + count))
    got = lane_select(both, at)
    turned = pltpu.roll(got, half, 0)
    from_left, from_right = jnp.where(low, got, turned), jnp.where(low, turned, got)
    tiles = elements // 128
    a, b = jnp.concatenate([ends_ref[0]] * tiles, axis=1), jnp.concatenate([ends_ref[1]] * tiles, axis=1)
    total = local_ref[:nc, :] + PENALTY * (a * from_left + b * from_right)
    out_ref[:nc, :] = total / c_ref[...]
    out_ref[nc:, :] = local_ref[nc:, :]


def end_kernel(nodes, x_ref, lift_ref, *refs):
    parts, (out_hbm, out_ref, sem) = refs[:-3], refs[-3:]
    n, p = nodes.n, nodes.p
    every = jnp.concatenate([ref[...] for ref in parts], axis=0)
    lifted = product(both_pieces(lift_ref), pieces(every))
    rows = x_ref.shape[1]
    size = n // p
    copies = []
    for s in range(rows // n):
        for r in range(0, n, 8):
            at = s * n + r
            to_halves(out_ref, at // p, load(x_ref, at, at + 8) + lifted[r : r + 8, :])
        here = pl.ds(s * size, size)
        copies.append(pltpu.make_async_copy(out_ref.at[here], out_hbm.at[here], sem.at[s]))
        copies[-1].start()
    for copy in copies:
        copy.wait()


def call(kernel, args, outs, scratch=(), hbm_in=False, hbm_out=False):
    spaces = [pltpu.HBM if flag else pltpu.VMEM for flag in (hbm_in, hbm_out)]
    return pl.pallas_call(
        kernel,
        out_shape=[jax.ShapeDtypeStruct(shape, dtype) for shape, dtype in outs],
        in_specs=[pl.BlockSpec(memory_space=spaces[0])] * len(args),
        out_specs=[pl.BlockSpec(memory_space=spaces[1])] * len(outs),
        scratch_shapes=scratch,
        compiler_params=pltpu.CompilerParams(vmem_limit_bytes=VMEM_BYTES),
        name=kernel.func.__name__,
    )(*args)


def swapped(first, second):
    peers = lax.axis_size("space")
    pairs = [[], []]
    for i in range(peers - 1):
        pairs[i % 2] += [(i, i + 1), (i + 1, i)]
    return [lax.ppermute(v, "space", q) for v, q in zip((first, second), pairs)]


def handed_on(last):
    peers = lax.axis_size("slab")
    return [lax.ppermute(last, "slab", [(i, i + 1) for i in range(k, peers - 1, 2)]) for k in (0, 1)]


def earlier(mine):
    peers = lax.axis_size("slab")
    parts = [mine]
    for k in range(1, peers):
        pairs = [(sources_of(i, peers)[k], i) for i in range(peers)]
        parts.append(lax.ppermute(mine, "slab", [(a, b) for a, b in pairs if 0 <= a < b]))
    return parts


def body(
    forcing, coefficient, neighbours, halo_faces, time_block, space_block, stiffness, time_restrict, space_restrict,
    coarse_smoother,
):
    slabs, q, p = forcing.shape[:3]
    elements = forcing.shape[-1]
    peers = lax.axis_size("slab")
    nodes = Nodes(q, p, space_restrict.shape[0])
    n, nc = nodes.n, nodes.nc
    rows = slabs * n
    count = halo_faces.shape[-1]
    tiles = elements // 128
    halves = (rows // p, tiles * p, 128)
    f = forcing.reshape(rows // p, p, tiles, 128).transpose(0, 2, 1, 3).reshape(halves)
    field = ((tiles, rows, 128), F32)
    face = ((rows // p, count), F32)
    plane = ((p**3, elements), F32)
    small = (time_block, space_block, stiffness, time_restrict, space_restrict, coarse_smoother)
    (
        x1, first, second, last, rf, c, nb, halo, inverse, step, coarse, lift, spread, ends
    ) = call(
        functools.partial(start_kernel, nodes, peers),
        (f, coefficient.reshape(1, elements), neighbours, halo_faces) + small,
        (
            field, face, face, plane, ((nc, elements), F32), ((1, elements), F32), (neighbours.shape, jnp.int32),
            (halo_faces.shape, jnp.int32), ((2, n, n), BF16), ((2, 2 * n, n), BF16), ((2, 3 * nc + nodes.nf, n), BF16),
            ((2, n, 2 * nc * peers), BF16), ((nc, nodes.nf), F32), ((2, 8, 128), F32),
        ),
        [pltpu.VMEM(halves, F32)]
        + [pltpu.SMEM(v.shape, F32) for v in small]
        + [pltpu.SemaphoreType.DMA((len(small),)), pltpu.SemaphoreType.DMA((3,)), pltpu.SemaphoreType.DMA((slabs,))],
        hbm_in=True,
    )
    x = x1
    for sweep in range(SWEEPS - 1):
        got = swapped(first, second) + handed_on(last)
        base, g = call(functools.partial(local_kernel, nodes), (x, x1, c, nb, step), (field, field))
        args = (base, g, *got, c, nb, inverse, halo)
        if sweep < SWEEPS - 2:
            x, first, second, last = call(functools.partial(finish_kernel, nodes), args, (field, face, face, plane))
        else:
            x, packed, local = call(
                functools.partial(coarse_kernel, nodes), args + (coarse, spread, rf),
                (field, ((8, count), F32), ((2 * nc, elements), F32)),
            )
    got = swapped(packed, packed)
    (mine,) = call(
        functools.partial(group_kernel, nodes), (local, *got, c, nb, ends), (((2 * nc, elements), F32),)
    )
    (out,) = call(
        functools.partial(end_kernel, nodes), (x, lift, *earlier(mine)), ((halves, F32),),
        [pltpu.VMEM(halves, F32), pltpu.SemaphoreType.DMA((slabs,))], hbm_out=True,
    )
    out = out.reshape(rows // p, tiles, p, 128).transpose(0, 2, 1, 3)
    return out.reshape(forcing.shape)


def solution(mesh):
    in_specs = (
        P("slab", None, None, None, None, "space"),
        P("space"),
        P(None, "space"),
        P(None, "space"),
        P(),
        P(),
        P(),
        P(),
        P(),
        P(),
    )
    out_specs = P("slab", None, None, None, None, "space")
    return jax.shard_map(body, mesh=mesh, in_specs=in_specs, out_specs=out_specs, check_vma=False)
```

```python
import functools

import jax
import jax.numpy as jnp
from jax import lax
from jax.experimental import pallas as pl
from jax.experimental.pallas import tpu as pltpu
from jax.sharding import PartitionSpec as P

SWEEPS = 3
PENALTY = 0.3
UPWIND = 0.5
COARSE_UPWIND = 0.6
F32 = jnp.float32
BF16 = jnp.bfloat16
VMEM_BYTES = 28 * 1024 * 1024


def iota(shape, dim):
    return lax.broadcasted_iota(jnp.int32, shape, dim)


def quotient(v, k):
    if k & (k - 1) == 0:
        return v >> (k.bit_length() - 1)
    return v // k


def digit(v, k, n):
    return quotient(v, k) & (n - 1) if n & (n - 1) == 0 else quotient(v, k) % n


def scalars(ref):
    return [[ref[i, j] for j in range(ref.shape[1])] for i in range(ref.shape[0])]


def two_minus(small):
    return [[(2.0 if i == j else 0.0) - v for j, v in enumerate(row)] for i, row in enumerate(small)]


def transposed(small):
    return [list(row) for row in zip(*small)]


def small_product(a, b):
    return [[sum(a[i][k] * b[k][j] for k in range(len(b))) for j in range(len(b[0]))] for i in range(len(a))]


def pick(at, values):
    out = jnp.zeros(at.shape, F32) + values[-1]
    for k in range(len(values) - 2, -1, -1):
        out = jnp.where(at == k, values[k], out)
    return out


def combine(left, rows):
    outs = []
    for line in left:
        total = line[0] * rows[0]
        for k in range(1, len(rows)):
            total = total + line[k] * rows[k]
        outs.append(total)
    return outs


def row_select(vectors, which, masks):
    columns = vectors[0].shape[-1]
    distinct = sorted(set(which))
    out = jnp.broadcast_to(vectors[distinct[0]], (8, columns))
    for v in distinct[1:]:
        here = tuple(i for i in range(8) if which[i] == v)
        if (here, columns) not in masks:
            sub = iota((8, columns), 0)
            mask = sub == here[0]
            for i in here[1:]:
                mask = jnp.logical_or(mask, sub == i)
            masks[here, columns] = mask
        out = jnp.where(masks[here, columns], vectors[v], out)
    return out


class Nodes:
    def __init__(self, q, p, pc):
        self.q, self.p, self.pc = q, p, pc
        self.n = q * p**3
        self.nc = pc**3
        self.nf = 6 * pc**2
        self.masks = {}

    def fresh(self):
        return Nodes(self.q, self.p, self.pc)

    def fine(self, d, r):
        return quotient(r, self.p**3) if d == 0 else digit(r, self.p ** (3 - d), self.p)

    def coarse(self, d, r):
        return digit(r, self.pc ** (3 - d), self.pc)

    def bit(self, d, face, r):
        pc = self.pc
        if d == 1:
            return digit(r, pc, pc)
        if d == 3:
            return digit(r, 1, pc)
        return jnp.where(face < 2, digit(r, pc, pc), digit(r, 1, pc))

    def over_fine(self, small, d):
        at = self.fine(d, iota((1, self.n), 1))
        return [pick(at, line) for line in small]

    def rows_of(self, count, factors):
        parts = []
        for g in range(0, count, 8):
            total = None
            for vectors, row_digit in factors:
                term = row_select(vectors, [row_digit(g + i) for i in range(8)], self.masks)
                total = term if total is None else total * term
            parts.append(total)
        return jnp.concatenate(parts, axis=0) if len(parts) > 1 else parts[0]

    def fine_rows(self, time, x, y, z):
        return self.rows_of(
            self.n, [(v, functools.partial(self.fine, d)) for d, v in enumerate((time, x, y, z))]
        )

    def coarse_rows(self, time, x, y, z):
        return self.rows_of(
            self.nc,
            [(time, lambda r: 0)] + [(v, functools.partial(self.coarse, d)) for d, v in ((1, x), (2, y), (3, z))],
        )

    def kron(self, time, x, y, z):
        return self.fine_rows(*(self.over_fine(v, d) for d, v in enumerate((time, x, y, z))))

    def restricted(self, time, space):
        return self.coarse_rows(*(self.over_fine(v, d) for d, v in enumerate((time, space, space, space))))

    def lifted(self, time, space, smoother, mine, sources):
        width = 2 * self.nc
        col = iota((1, width * len(sources)), 1)
        block = quotient(col, width)
        owner = jnp.zeros_like(col) + sources[0]
        for k in range(1, len(sources)):
            owner = jnp.where(block == k, sources[k], owner)
        steps = mine - owner - digit(col, self.nc, 2)
        power, decay, powers, decays = smoother, 1.0, [], []
        for _ in sources:
            powers.append(small_product(transposed(space), power))
            decays.append(decay)
            power, decay = small_product(power, smoother), decay * COARSE_UPWIND
        weight = jnp.where(steps < 0, 0.0, pick(steps, decays))
        factors = [[weight * v for v in time[0]]]
        for d in (1, 2, 3):
            at = self.coarse(d, col)
            factors.append(
                [pick(at, [pick(steps, [z[x][i] for z in powers]) for i in range(self.pc)]) for x in range(self.p)]
            )
        return self.fine_rows(*factors)

    def face_traces(self, time, space):
        four, pc, p = self.pc**2, self.pc, self.p
        factors = [(self.over_fine(time, 0), lambda r: 0)]
        for d in (1, 2, 3):
            at = self.fine(d, iota((1, self.n), 1))
            vectors = self.over_fine(space, d)
            vectors = vectors + [(at == node).astype(F32) for node in (p - 1, 0)]

            def row_digit(r, d=d):
                face, high, low = r // four, r // pc % pc, r % pc
                if face // 2 == d - 1:
                    return pc + face % 2
                return high if d == 1 or (d == 2 and face < 2) else low

            factors.append((vectors, row_digit))
        return self.rows_of(self.nf, factors)

    def face_spread(self, space):
        col = iota((1, self.nf), 1)
        face = quotient(col, self.pc**2)
        factors = []
        for d in (1, 2, 3):
            vectors = []
            for i in range(self.pc):
                normal = jnp.where(digit(face, 1, 2) == 0, space[i][0], space[i][self.p - 1])
                tangential = (self.bit(d, face, col) == i).astype(F32)
                vectors.append(jnp.where(quotient(face, 2) == d - 1, normal, tangential))
            factors.append((vectors, functools.partial(self.coarse, d)))
        return self.rows_of(self.nc, factors)


def pieces(v):
    high = v.astype(BF16)
    return high, (v - high.astype(F32)).astype(BF16)


def bdot(a, b):
    return jnp.dot(a, b, preferred_element_type=F32)


def product(matrix, values):
    mh, ml = matrix
    vh, vl = values
    return bdot(mh, vh) + (bdot(mh, vl) + bdot(ml, vh))


def lane_select(values, indices):
    outs = []
    for j in range(0, indices.shape[-1], 128):
        at = indices[:, j : j + 128]
        tile, lane = at >> 7, at & 127
        out = jnp.zeros(at.shape, F32)
        for k in range(values.shape[-1] // 128):
            got = jnp.take_along_axis(values[:, 128 * k : 128 * k + 128], lane, axis=1, mode="promise_in_bounds")
            out = jnp.where(tile == k, got, out)
        outs.append(out)
    return jnp.concatenate(outs, axis=1)


def select_columns(values, indices, count):
    rows = values.shape[0]
    high, low = pieces(values)
    chosen = (iota((count, indices.shape[-1]), 0) == indices).astype(F32).astype(BF16)
    both = bdot(jnp.concatenate([high, low], axis=0), chosen)
    return both[:rows] + both[rows:]


def lower_half(shape):
    return iota(shape, 0) < 4


def load(ref, start, stop):
    return jnp.concatenate([ref[k, start:stop, :] for k in range(ref.shape[0])], axis=1)


def store(ref, start, values):
    for k in range(ref.shape[0]):
        ref[k, start : start + values.shape[0], :] = values[:, 128 * k : 128 * k + 128]


def accumulate(ref, start, values):
    for k in range(ref.shape[0]):
        ref[k, start : start + values.shape[0], :] += values[:, 128 * k : 128 * k + 128]


def trace_rows(ref, face, p):
    rows = ref.shape[1]
    d, node = face // 2, face % 2 * (p - 1)
    if d == 0:
        step = p * p
        parts = [load(ref, r + node * step, r + (node + 1) * step) for r in range(0, rows, p * step)]
        return jnp.concatenate(parts, axis=0)
    if d == 1:
        parts = []
        at = node * p // 8 * 8
        for r in range(0, rows, 2 * p * p):
            first = load(ref, r + at, r + at + 8)
            second = load(ref, r + p * p + at, r + p * p + at + 8)
            low = lower_half(first.shape)
            if node == 0:
                parts.append(jnp.where(low, first, pltpu.roll(second, 4, 0)))
            else:
                parts.append(jnp.where(low, pltpu.roll(first, 4, 0), second))
        return jnp.concatenate(parts, axis=0)
    parts = [ref[k, pl.ds(node, rows // p, stride=p), :] for k in range(ref.shape[0])]
    return jnp.concatenate(parts, axis=1)


def add_rows(ref, values, face, p):
    rows = ref.shape[1]
    d, node = face // 2, face % 2 * (p - 1)
    if d == 0:
        step = p * p
        for i, r in enumerate(range(0, rows, p * step)):
            accumulate(ref, r + node * step, values[i * step : (i + 1) * step])
    elif d == 1:
        at = node * p // 8 * 8
        for i, r in enumerate(range(0, rows, 2 * p * p)):
            eight = values[8 * i : 8 * i + 8]
            turned = pltpu.roll(eight, 4, 0)
            low = lower_half(eight.shape)
            if node == 0:
                first, second = jnp.where(low, eight, 0.0), jnp.where(low, turned, 0.0)
            else:
                first, second = jnp.where(low, 0.0, turned), jnp.where(low, 0.0, eight)
            accumulate(ref, r + at, first)
            accumulate(ref, r + p * p + at, second)
    else:
        for k in range(ref.shape[0]):
            where = (k, pl.ds(node, rows // p, stride=p), slice(None))
            ref[where] = ref[where] + values[:, 128 * k : 128 * k + 128]


def from_halves(ref, row):
    tiles = []
    for k in range(0, ref.shape[1], 8):
        first, second = ref[row, k : k + 8, :], ref[row + 1, k : k + 8, :]
        low = lower_half(first.shape)
        tiles.append(jnp.where(low, first, pltpu.roll(second, 4, 0)))
        tiles.append(jnp.where(low, pltpu.roll(first, 4, 0), second))
    return jnp.concatenate(tiles, axis=1)


def to_halves(ref, row, values):
    for k in range(0, ref.shape[1], 8):
        at = 32 * k
        first, second = values[:, at : at + 128], values[:, at + 128 : at + 256]
        low = lower_half(first.shape)
        ref[row, k : k + 8, :] = jnp.where(low, first, pltpu.roll(second, 4, 0))
        ref[row + 1, k : k + 8, :] = jnp.where(low, pltpu.roll(first, 4, 0), second)


def keep_pieces(ref, matrix):
    high, low = pieces(matrix)
    ref[0] = high
    ref[1] = low


def both_pieces(ref):
    return ref[0], ref[1]


def last_time(nodes):
    return (nodes.q - 1) * nodes.p**3


def is_even():
    return lax.axis_index("space") % 2 == 0


def pack(x_ref, halo_ref, first_ref, second_ref, p):
    elements = x_ref.shape[0] * 128
    to_left = select_columns(trace_rows(x_ref, 0, p), halo_ref[0:1, :], elements)
    to_right = select_columns(trace_rows(x_ref, 1, p), halo_ref[1:2, :], elements)
    even = is_even()
    first_ref[...] = jnp.where(even, to_right, to_left)
    second_ref[...] = jnp.where(even, to_left, to_right)


def sources_of(mine, peers):
    if peers & (peers - 1) == 0:
        return [mine ^ k for k in range(peers)]
    return [mine - k for k in range(peers)]


def start_kernel(
    nodes, peers, f_hbm, c_hbm, nb_hbm, halo_hbm, tb_hbm, sb_hbm, st_hbm, tr_hbm, sr_hbm, cs_hbm,
    x_ref, first_ref, second_ref, last_ref, rf_ref, c_ref, nb_ref, halo_ref,
    inverse_ref, step_ref, coarse_ref, lift_ref, spread_ref, ends_ref,
    f_ref, tb, sb, st, tr, sr, cs, small_sem, table_sem, field_sem,
):
    nodes = nodes.fresh()
    n, p, nc = nodes.n, nodes.p, nodes.nc
    rows = x_ref.shape[1]
    small = [(tb_hbm, tb), (sb_hbm, sb), (st_hbm, st), (tr_hbm, tr), (sr_hbm, sr), (cs_hbm, cs)]
    tables = [(c_hbm, c_ref), (nb_hbm, nb_ref), (halo_hbm, halo_ref)]
    small = [pltpu.make_async_copy(a, b, small_sem.at[i]) for i, (a, b) in enumerate(small)]
    tables = [pltpu.make_async_copy(a, b, table_sem.at[i]) for i, (a, b) in enumerate(tables)]
    slabs = rows // n
    size = n // p
    fields = [
        pltpu.make_async_copy(f_hbm.at[pl.ds(s * size, size)], f_ref.at[pl.ds(s * size, size)], field_sem.at[s])
        for s in range(slabs)
    ]
    for copy in small + fields + tables:
        copy.start()
    for copy in small:
        copy.wait()
    t, b, d, tt, ss, w = (scalars(ref) for ref in (tb, sb, st, tr, sr, cs))
    ti, si = two_minus(t), two_minus(b)
    et = nodes.over_fine(ti, 0)
    es = [nodes.over_fine(si, k) for k in (1, 2, 3)]
    of_b = [nodes.over_fine(b, k) for k in (1, 2, 3)]
    of_d = [nodes.over_fine(d, k) for k in (1, 2, 3)]
    of_t = nodes.over_fine(t, 0)
    inverse = pieces(nodes.fine_rows(et, *es))
    inverse_ref[0], inverse_ref[1] = inverse
    unit = (iota((n, n), 0) == iota((n, n), 1)).astype(F32)
    keep = unit - nodes.fine_rows(combine(ti, of_t), *(combine(si, v) for v in of_b))
    ed = [combine(si, v) for v in of_d]
    drift = nodes.fine_rows(et, ed[0], es[1], es[2]) + nodes.fine_rows(et, es[0], ed[1], es[2])
    drift = -(drift + nodes.fine_rows(et, es[0], es[1], ed[2]))
    keep_pieces(step_ref, jnp.concatenate([keep, drift], axis=0))
    rt = nodes.over_fine(tt, 0)
    rs = [nodes.over_fine(ss, k) for k in (1, 2, 3)]
    rd = [combine(ss, v) for v in of_d]
    block = nodes.coarse_rows(combine(tt, of_t), *(combine(ss, v) for v in of_b))
    stiff = nodes.coarse_rows(rt, rd[0], rs[1], rs[2]) + nodes.coarse_rows(rt, rs[0], rd[1], rs[2])
    stiff = stiff + nodes.coarse_rows(rt, rs[0], rs[1], rd[2])
    restrict = nodes.coarse_rows(rt, *rs)
    keep_pieces(coarse_ref, jnp.concatenate([restrict, block, stiff, nodes.face_traces(tt, ss)], axis=0))
    mine = lax.axis_index("slab")
    keep_pieces(lift_ref, nodes.lifted(tt, ss, w, mine, sources_of(mine, peers)))
    spread_ref[...] = nodes.face_spread(ss)
    sub = iota((8, 128), 0)
    half = nodes.pc**2
    ends_ref[0] = jnp.where(sub < half, ss[0][0], ss[1][0])
    ends_ref[1] = jnp.where(sub < half, ss[0][p - 1], ss[1][p - 1])
    tables[0].wait()
    scale = 1.0 / c_ref[...]
    total = 0.0
    for s in range(slabs):
        fields[s].wait()
        f = jnp.concatenate([from_halves(f_ref, (s * n + r) // p) for r in range(0, n, 8)], axis=0)
        total = total + f
        store(x_ref, s * n, product(inverse, pieces(f)) * scale)
    tables[1].wait()
    tables[2].wait()
    pack(x_ref, halo_ref, first_ref, second_ref, p)
    last_ref[...] = load(x_ref, rows - n + last_time(nodes), rows)
    high, low = pieces(restrict)
    rf_ref[...] = product((high, low), pieces(total))


def local_kernel(nodes, x_ref, x1_ref, c_ref, nb_ref, step_ref, base_ref, g_ref):
    n, p = nodes.n, nodes.p
    rows = x_ref.shape[1]
    elements = x_ref.shape[0] * 128
    c = c_ref[...]
    scale = 1.0 / c
    g_ref[...] = jnp.zeros_like(g_ref)
    for s in range(1, rows // n):
        before = (s - 1) * n + last_time(nodes)
        store(g_ref, s * n, UPWIND * c * load(x_ref, before, before + p**3))
    step = both_pieces(step_ref)
    for face in range(6):
        values = trace_rows(x_ref, face ^ 1, p)
        add_rows(g_ref, PENALTY * select_columns(values, nb_ref[face : face + 1, :], elements), face, p)
    for s in range(rows // n):
        moved = product(step, pieces(load(x_ref, s * n, (s + 1) * n)))
        store(base_ref, s * n, load(x1_ref, s * n, (s + 1) * n) + moved[:n] + scale * moved[n:])


def finish(nodes, base_ref, g_ref, got_first, got_second, prev_a, prev_b, c_ref, nb_ref, inverse_ref, x_ref):
    n, p = nodes.n, nodes.p
    rows = base_ref.shape[1]
    elements = base_ref.shape[0] * 128
    inverse = both_pieces(inverse_ref)
    c = c_ref[...]
    scale = 1.0 / c
    even = is_even()
    first, second = got_first[...], got_second[...]
    left, right = jnp.where(even, second, first), jnp.where(even, first, second)
    count = left.shape[-1]
    left = PENALTY * select_columns(left, nb_ref[0:1, :] - elements, count)
    right = PENALTY * select_columns(right, nb_ref[1:2, :] - (elements + count), count)
    handed = (UPWIND * c) * (prev_a[...] + prev_b[...])
    step = p * p
    for s in range(rows // n):
        parts = []
        for time in range(nodes.q):
            at = (s * nodes.q + time) * step
            for x in range(p):
                start = s * n + time * p**3 + x * step
                part = load(g_ref, start, start + step)
                if x == 0:
                    part = part + left[at : at + step]
                if x == p - 1:
                    part = part + right[at : at + step]
                if s == 0 and time == 0:
                    part = part + handed[x * step : (x + 1) * step]
                parts.append(part)
        moved = product(inverse, pieces(jnp.concatenate(parts, axis=0)))
        store(x_ref, s * n, load(base_ref, s * n, (s + 1) * n) + scale * moved)


def finish_kernel(
    nodes, base_ref, g_ref, got_first, got_second, prev_a, prev_b, c_ref, nb_ref, inverse_ref, halo_ref,
    x_ref, first_ref, second_ref, last_ref,
):
    finish(nodes, base_ref, g_ref, got_first, got_second, prev_a, prev_b, c_ref, nb_ref, inverse_ref, x_ref)
    rows = base_ref.shape[1]
    pack(x_ref, halo_ref, first_ref, second_ref, nodes.p)
    last_ref[...] = load(x_ref, rows - nodes.n + last_time(nodes), rows)


def coarse_kernel(
    nodes, base_ref, g_ref, got_first, got_second, prev_a, prev_b, c_ref, nb_ref, inverse_ref, halo_ref,
    coarse_ref, spread_ref, rf_ref,
    x_ref, packed_ref, local_ref,
):
    finish(nodes, base_ref, g_ref, got_first, got_second, prev_a, prev_b, c_ref, nb_ref, inverse_ref, x_ref)
    n, p, nc = nodes.n, nodes.p, nodes.nc
    rows = x_ref.shape[1]
    elements = x_ref.shape[0] * 128
    half = nodes.pc**2
    high, low = both_pieces(coarse_ref)
    total = load(x_ref, 0, n)
    before = 0.0
    for k in range(1, rows // n):
        total = total + load(x_ref, k * n, (k + 1) * n)
        at = (k - 1) * n + last_time(nodes)
        before = before + load(x_ref, at, at + p**3)
    applied = product((high, low), pieces(total))[nc:]
    traces = applied[2 * nc :]
    halo = halo_ref[...]
    packed_ref[...] = lane_select(
        traces[:8], jnp.where(iota((8, halo.shape[-1]), 0) < half, halo[1:2, :], halo[0:1, :])
    )
    low_half = iota((8, elements), 0) < half
    coupled = [
        lane_select(
            traces[8 * k : 8 * k + 8],
            jnp.where(low_half, nb_ref[2 * k : 2 * k + 1, :], nb_ref[2 * k + 1 : 2 * k + 2, :]),
        )
        for k in range(3)
    ]
    c = c_ref[...]
    end = load(x_ref, rows - n + last_time(nodes), rows)
    plane = p**3
    moved = product((high[:, :plane], low[:, :plane]), pieces(jnp.concatenate([before, end], axis=1)))[:nc]
    local = rf_ref[...] - c * applied[:nc] - applied[nc : 2 * nc] + (UPWIND * c) * moved[:, :elements]
    spread = product(pieces(spread_ref[...]), pieces(jnp.concatenate(coupled, axis=0)))
    local_ref[:nc, :] = local + PENALTY * spread
    local_ref[nc:, :] = UPWIND * moved[:, elements:]


def group_kernel(nodes, local_ref, got_first, got_second, c_ref, nb_ref, ends_ref, out_ref):
    nc = nodes.nc
    elements = local_ref.shape[-1]
    half = nodes.pc**2
    first, second = got_first[...], got_second[...]
    count = first.shape[-1]
    even = is_even()
    left, right = jnp.where(even, second, first), jnp.where(even, first, second)
    both = jnp.where(iota((8, count), 0) < half, left, right)
    low = iota((8, elements), 0) < half
    at = jnp.where(low, nb_ref[0:1, :] - elements, nb_ref[1:2, :] - (elements + count))
    got = lane_select(both, at)
    turned = pltpu.roll(got, half, 0)
    from_left, from_right = jnp.where(low, got, turned), jnp.where(low, turned, got)
    tiles = elements // 128
    a, b = jnp.concatenate([ends_ref[0]] * tiles, axis=1), jnp.concatenate([ends_ref[1]] * tiles, axis=1)
    total = local_ref[:nc, :] + PENALTY * (a * from_left + b * from_right)
    out_ref[:nc, :] = total / c_ref[...]
    out_ref[nc:, :] = local_ref[nc:, :]


def end_kernel(nodes, x_ref, lift_ref, *refs):
    parts, (out_hbm, out_ref, sem) = refs[:-3], refs[-3:]
    n, p = nodes.n, nodes.p
    every = jnp.concatenate([ref[...] for ref in parts], axis=0)
    lifted = product(both_pieces(lift_ref), pieces(every))
    rows = x_ref.shape[1]
    size = n // p
    copies = []
    for s in range(rows // n):
        for r in range(0, n, 8):
            at = s * n + r
            to_halves(out_ref, at // p, load(x_ref, at, at + 8) + lifted[r : r + 8, :])
        here = pl.ds(s * size, size)
        copies.append(pltpu.make_async_copy(out_ref.at[here], out_hbm.at[here], sem.at[s]))
        copies[-1].start()
    for copy in copies:
        copy.wait()


def call(kernel, args, outs, scratch=(), hbm_in=False, hbm_out=False):
    spaces = [pltpu.HBM if flag else pltpu.VMEM for flag in (hbm_in, hbm_out)]
    return pl.pallas_call(
        kernel,
        out_shape=[jax.ShapeDtypeStruct(shape, dtype) for shape, dtype in outs],
        in_specs=[pl.BlockSpec(memory_space=spaces[0])] * len(args),
        out_specs=[pl.BlockSpec(memory_space=spaces[1])] * len(outs),
        scratch_shapes=scratch,
        compiler_params=pltpu.CompilerParams(vmem_limit_bytes=VMEM_BYTES),
        name=kernel.func.__name__,
    )(*args)


def swapped(first, second):
    peers = lax.axis_size("space")
    pairs = [[], []]
    for i in range(peers - 1):
        pairs[i % 2] += [(i, i + 1), (i + 1, i)]
    return [lax.ppermute(v, "space", q) for v, q in zip((first, second), pairs)]


def handed_on(last):
    peers = lax.axis_size("slab")
    return [lax.ppermute(last, "slab", [(i, i + 1) for i in range(k, peers - 1, 2)]) for k in (0, 1)]


def earlier(mine):
    peers = lax.axis_size("slab")
    parts = [mine]
    for k in range(1, peers):
        pairs = [(sources_of(i, peers)[k], i) for i in range(peers)]
        parts.append(lax.ppermute(mine, "slab", [(a, b) for a, b in pairs if 0 <= a < b]))
    return parts


def body(
    forcing, coefficient, neighbours, halo_faces, time_block, space_block, stiffness, time_restrict, space_restrict,
    coarse_smoother,
):
    slabs, q, p = forcing.shape[:3]
    elements = forcing.shape[-1]
    peers = lax.axis_size("slab")
    nodes = Nodes(q, p, space_restrict.shape[0])
    n, nc = nodes.n, nodes.nc
    rows = slabs * n
    count = halo_faces.shape[-1]
    tiles = elements // 128
    halves = (rows // p, tiles * p, 128)
    f = forcing.reshape(rows // p, p, tiles, 128).transpose(0, 2, 1, 3).reshape(halves)
    field = ((tiles, rows, 128), F32)
    face = ((rows // p, count), F32)
    plane = ((p**3, elements), F32)
    small = (time_block, space_block, stiffness, time_restrict, space_restrict, coarse_smoother)
    (
        x1, first, second, last, rf, c, nb, halo, inverse, step, coarse, lift, spread, ends
    ) = call(
        functools.partial(start_kernel, nodes, peers),
        tuple(
            pltpu.with_memory_space_constraint(v, pltpu.HBM)
            for v in (f, coefficient.reshape(1, elements), neighbours, halo_faces) + small
        ),
        (
            field, face, face, plane, ((nc, elements), F32), ((1, elements), F32), (neighbours.shape, jnp.int32),
            (halo_faces.shape, jnp.int32), ((2, n, n), BF16), ((2, 2 * n, n), BF16), ((2, 3 * nc + nodes.nf, n), BF16),
            ((2, n, 2 * nc * peers), BF16), ((nc, nodes.nf), F32), ((2, 8, 128), F32),
        ),
        [pltpu.VMEM(halves, F32)]
        + [pltpu.SMEM(v.shape, F32) for v in small]
        + [pltpu.SemaphoreType.DMA((len(small),)), pltpu.SemaphoreType.DMA((3,)), pltpu.SemaphoreType.DMA((slabs,))],
        hbm_in=True,
    )
    x = x1
    for sweep in range(SWEEPS - 1):
        got = swapped(first, second) + handed_on(last)
        base, g = call(functools.partial(local_kernel, nodes), (x, x1, c, nb, step), (field, field))
        args = (base, g, *got, c, nb, inverse, halo)
        if sweep < SWEEPS - 2:
            x, first, second, last = call(functools.partial(finish_kernel, nodes), args, (field, face, face, plane))
        else:
            x, packed, local = call(
                functools.partial(coarse_kernel, nodes), args + (coarse, spread, rf),
                (field, ((8, count), F32), ((2 * nc, elements), F32)),
            )
    got = swapped(packed, packed)
    (mine,) = call(
        functools.partial(group_kernel, nodes), (local, *got, c, nb, ends), (((2 * nc, elements), F32),)
    )
    (out,) = call(
        functools.partial(end_kernel, nodes), (x, lift, *earlier(mine)), ((halves, F32),),
        [pltpu.VMEM(halves, F32), pltpu.SemaphoreType.DMA((slabs,))], hbm_out=True,
    )
    out = out.reshape(rows // p, tiles, p, 128).transpose(0, 2, 1, 3)
    return out.reshape(forcing.shape)


def solution(mesh):
    in_specs = (
        P("slab", None, None, None, None, "space"),
        P("space"),
        P(None, "space"),
        P(None, "space"),
        P(),
        P(),
        P(),
        P(),
        P(),
        P(),
    )
    out_specs = P("slab", None, None, None, None, "space")
    return jax.shard_map(body, mesh=mesh, in_specs=in_specs, out_specs=out_specs, check_vma=False)
```
